32 devices in a mesh: groups: 2 (over y), wide: 4 (over z), narrow: 4 (over x, core).
Axes of the slice: x: 2, y: 2, z: 4, core: 2. Of those that a mesh axis runs over, the one named last changes fastest.
Arguments:
- hidden: bfloat16 [32, 8192], P('groups', 'wide'), parts along dimension 0, may hold values from -6 to 6
- w_query: bfloat16 [8192, 8192], P('wide', 'narrow'), may hold values from -0.0625 to 0.0625
- w_key: bfloat16 [8192, 1024], P('wide', 'narrow'), may hold values from -0.0625 to 0.0625
- w_value: bfloat16 [8192, 1024], P('wide', 'narrow'), may hold values from -0.0625 to 0.0625
- w_out: bfloat16 [8192, 8192], P('narrow', 'wide'), may hold values from -0.0625 to 0.0625
- key_cache: bfloat16 [32, 768, 8, 128], P(('groups', 'wide'), None, 'narrow'), parts along dimension 0, may hold values from -720 to 720
- value_cache: bfloat16 [32, 768, 8, 128], P(('groups', 'wide'), None, 'narrow'), parts along dimension 0, may hold values from -6 to 6
- cycle_offset: int32 [32], P(('groups', 'wide')), parts along dimension 0, may hold values from 0 to 767
- valid_length: int32 [32], P(('groups', 'wide')), parts along dimension 0, may hold values from 1 to 768, as said below
- slot_of: int32 [32], P('groups'), parts along dimension 0, may hold values from 0 to 15, as said below
Outputs:
- attn_out: bfloat16 [32, 8192], P('groups', 'wide'), parts along dimension 0
- new_keys: bfloat16 [32, 1024], P(('groups', 'wide'), 'narrow'), parts along dimension 0
- new_values: bfloat16 [32, 1024], P(('groups', 'wide'), 'narrow'), parts along dimension 0
The draws below stay inside these ranges and needn't reach their ends.
There are 2 independent parts, one for each index of `groups`. The reference program is written for one: setup_inputs(seed, part) draws one part's arguments, and reference() takes and returns one part's arrays. A program takes and returns all parts, laid end to end along the dimension named above; an argument that names none is the same for every part. Nothing has to cross between parts.
Inputs may be any that keep to these rules, and one draw needn't show every extreme that they name: Requests are in 4 microbatches of consecutive rows; each cache owner (a block of 4 consecutive slots) holds exactly 1 request of each microbatch m, at the slots owner * 4 + m + j for 0 <= j < 1; slot_of is a permutation. `valid_length`: at least one slot has a full cycle.
All inputs are finite; a program needn't handle non-finite values.
Results may differ from the reference program's by a relative error of at most 0.012.
Values may be sent and summed in bfloat16 or wider, within the bound.
A program may use at most 64 MiB of HBM per device.

```python
import jax
import jax.numpy as jnp
from jax import lax

D = 8192
HQ = 64
KV = 8
HD = 128
L = 768
SLOT_MB = 1
MICRO = 4
REQ_DEV = 4
REQUESTS = 16


def draw_key_cache(key, part):
    base = jax.random.normal(jax.random.fold_in(key, 11), (REQUESTS, L, KV, HD), jnp.float32)
    base = jnp.clip(base, -6.0, 6.0)
    return base.astype(jnp.bfloat16)


def draw_valid_length(key, part):
    lengths = jax.random.randint(jax.random.fold_in(key, 21), (REQUESTS,), 1, L + 1)
    longest = jax.random.randint(jax.random.fold_in(key, 22), (), 0, REQUESTS)
    return jnp.where(jnp.arange(REQUESTS, dtype=jnp.int32) == longest, L, lengths).astype(jnp.int32)


def draw_slot_of(key, part):
    rows_block = REQUESTS // MICRO
    block_keys = jax.random.split(jax.random.fold_in(key, 31), MICRO)

    def shuffle(one_key):
        return jax.random.permutation(one_key, rows_block)
    perms = jax.vmap(shuffle)(block_keys)
    blocks = jnp.arange(MICRO, dtype=jnp.int32)[:, None]
    owner = perms // SLOT_MB
    within = perms % SLOT_MB
    slots = owner * REQ_DEV + blocks * SLOT_MB + within
    return slots.reshape(REQUESTS).astype(jnp.int32)


def touch_ends(result, stream_key, least, top_value):
    shape = result.shape
    spot = [jax.random.randint(jax.random.fold_in(stream_key, axis), (), 0, shape[axis]) for axis in range(len(shape))]
    result = result.at[tuple(spot)].set(least)
    longest = shape.index(max(shape))
    spot[longest] = (spot[longest] + 1) % shape[longest]
    return result.at[tuple(spot)].set(top_value)


def level_of(stream_key, extent, pieces, least, high):
    def one(position, parts):
        heights = jax.random.uniform(jax.random.fold_in(jax.random.fold_in(stream_key, 6), position), (parts,), jnp.float32, least / len(pieces), high / len(pieces))
        return jnp.repeat(jnp.exp(heights), extent[position] // parts).reshape((-1,) + (1,) * (len(extent) - position - 1))

    gain = one(*pieces[0])
    for cut in pieces[1:]:
        gain = gain * one(*cut)
    return gain


def gaussian(own_key, shape, width, bound, pieces=(), kind=jnp.bfloat16):
    factor_of = level_of(own_key, shape, pieces, -0.22, 0.18) if pieces else 1.0
    values = jax.random.normal(own_key, shape, jnp.float32) * width * factor_of
    return jnp.minimum(jnp.maximum(values, -bound), bound).astype(kind)


def setup_inputs(seed: int = 0, part: int = 0) -> dict:
    splits = jax.random.split(jax.random.key(seed), 11)
    part_splits = jax.random.split(jax.random.fold_in(splits[10], part), 11)
    return {
        "hidden": gaussian(part_splits[0], (REQUESTS, D), 1.0, 6.0, ((1, 4),)),
        "w_query": gaussian(splits[1], (D, HQ * HD), D ** -0.5, 0.0625, ((0, 4), (1, 4))),
        "w_key": gaussian(splits[2], (D, KV * HD), D ** -0.5, 0.0625, ((0, 4), (1, 4))),
        "w_value": gaussian(splits[3], (D, KV * HD), D ** -0.5, 0.0625, ((0, 4), (1, 4))),
        "w_out": gaussian(splits[4], (HQ * HD, D), (HQ * HD) ** -0.5, 0.0625, ((0, 4), (1, 4))),
        "key_cache": draw_key_cache(jax.random.fold_in(jax.random.fold_in(splits[10], part), 71), part),
        "value_cache": gaussian(part_splits[6], (REQUESTS, L, KV, HD), 1.0, 6.0, ((0, 4), (2, 4))),
        "cycle_offset": touch_ends(jax.random.randint(part_splits[7], (REQUESTS,), 0, L), jax.random.fold_in(part_splits[7], 1), 0, L - 1).astype(jnp.int32),
        "valid_length": draw_valid_length(jax.random.fold_in(jax.random.fold_in(splits[10], part), 71), part),
        "slot_of": draw_slot_of(jax.random.fold_in(jax.random.fold_in(splits[10], part), 71), part),
    }


def reference(hidden, w_query, w_key, w_value, w_out, key_cache, value_cache, cycle_offset, valid_length, slot_of):
    order = jnp.zeros((REQUESTS,), jnp.int32).at[slot_of].set(jnp.arange(REQUESTS, dtype=jnp.int32))
    slot_rows = hidden[order]
    queries = jnp.dot(slot_rows, w_query, preferred_element_type=jnp.float32).astype(jnp.bfloat16)
    new_keys = jnp.dot(slot_rows, w_key, preferred_element_type=jnp.float32).astype(jnp.bfloat16)
    new_values = jnp.dot(slot_rows, w_value, preferred_element_type=jnp.float32).astype(jnp.bfloat16)
    group = HQ // KV
    scale = 1.0 / jnp.sqrt(jnp.float32(HD))

    def one_slot(items):
        query_row, key_row, value_row, keys_old, values_old, offset, length = items
        keys_all = keys_old.at[offset].set(key_row.reshape(KV, HD))
        values_all = values_old.at[offset].set(value_row.reshape(KV, HD))
        query_heads = query_row.reshape(KV, group, HD).astype(jnp.float32)
        scores = jnp.einsum('kgd,jkd->kgj', query_heads, keys_all.astype(jnp.float32)) * scale
        distance = (offset - jnp.arange(L, dtype=jnp.int32)) % L
        usable = (distance < length)[None, None, :]
        masked = jnp.where(usable, scores, -jnp.inf)
        top = lax.optimization_barrier(jnp.max(masked, axis=2, keepdims=True))
        spread = jnp.where(usable, jnp.exp(masked - top), 0.0)
        probs = (spread / lax.optimization_barrier(jnp.sum(spread, axis=2, keepdims=True))).astype(jnp.bfloat16)
        mixed = jnp.einsum('kgj,jkd->kgd', probs.astype(jnp.float32), values_all.astype(jnp.float32))
        return mixed.astype(jnp.bfloat16).reshape(HQ * HD)
    heads = lax.map(one_slot, (queries, new_keys, new_values, key_cache, value_cache, cycle_offset, valid_length))
    projected = jnp.dot(heads, w_out, preferred_element_type=jnp.float32)
    attn_out = projected[slot_of].astype(jnp.bfloat16)
    return (attn_out, new_keys, new_values)
```

```python
import functools

import jax
import jax.numpy as jnp
from jax import lax
from jax.experimental import pallas as pl
from jax.experimental.pallas import tpu as pltpu
from jax.sharding import PartitionSpec as P

masked_low = -1e30
scope = jax.named_scope
MESH = pl.DeviceIdType.MESH
head_parts = (2, 2)
finish_kib = 1024
main_kib = 64512
o_most = 1024
ahead = 4


def width_of(columns, most):
    width = min(columns, most)
    while columns % width:
        width -= 128
    return width


def blocks_of(columns, kv_local, wide):
    per_head = columns // kv_local
    result = []
    for k in range(kv_local):
        parts = head_parts[min(k, len(head_parts) - 1)] if wide <= 8 else 1
        width = width_of(per_head, max(per_head // parts // 128 * 128, 128))
        result += [(k * per_head + col, width) for col in range(0, per_head, width)]
    return tuple(result)


def kernel(
    wide,
    narrow,
    kv_local,
    q_blocks,
    o_width,
    hidden_in,
    w_query,
    w_key,
    w_value,
    w_out,
    key_cache,
    value_cache,
    slot_row_in,
    cycle_offset_in,
    valid_length_in,
    attn_out,
    new_keys,
    new_values,
    hidden,
    slot_row,
    cycle_offset,
    valid_length,
    wq,
    wk,
    wv,
    wo,
    keys,
    values,
    part,
    got,
    queries,
    bias,
    heads_own,
    heads_got,
    heads_full,
    out_early,
    out_part,
    out_got,
    in_sem,
    small_sem,
    send_sem,
    recv_sem,
):
    me_wide = lax.axis_index("wide")
    me_narrow = lax.axis_index("narrow")
    requests = hidden.shape[0]
    slots = keys.shape[0]
    head_dim = keys.shape[2]
    span = keys.shape[1]
    window = span // kv_local
    query_cols = wq.shape[1]
    key_cols = wk.shape[1]
    out_cols = wo.shape[1]
    heads_local = query_cols // head_dim
    group = heads_local // kv_local
    group_cols = group * head_dim
    q_chunks = len(q_blocks)
    o_chunks = out_cols // o_width

    first = [
        pltpu.make_async_copy(w_key, wk, in_sem.at[0]),
        pltpu.make_async_copy(w_value, wv, in_sem.at[1]),
    ]
    for c, (col, width) in enumerate(q_blocks):
        cols = pl.ds(col, width)
        first.append(pltpu.make_async_copy(w_query.at[:, cols], wq.at[:, cols], in_sem.at[2 + c]))
    base = 2 + q_chunks
    cache_in = [
        pltpu.make_async_copy(key_cache, keys, in_sem.at[base]),
        pltpu.make_async_copy(value_cache, values, in_sem.at[base + 1]),
    ]
    out_in = []
    for k in range(kv_local):
        span_k = pl.ds(k * group_cols, group_cols)
        out_in.append(
            pltpu.make_async_copy(w_out.at[span_k], wo.at[span_k], in_sem.at[base + 2 + k])
        )
    small = [
        pltpu.make_async_copy(hidden_in, hidden, small_sem.at[0]),
        pltpu.make_async_copy(slot_row_in, slot_row, small_sem.at[1]),
        pltpu.make_async_copy(cycle_offset_in, cycle_offset, small_sem.at[2]),
        pltpu.make_async_copy(valid_length_in, valid_length, small_sem.at[3]),
    ]
    stream = first + cache_in + out_in
    for copy in small[:2] + stream[:ahead] + small[2:]:
        copy.start()

    barrier = pltpu.get_barrier_semaphore()
    peers = wide + narrow - 2
    for d in range(1, wide):
        pl.semaphore_signal(
            barrier,
            inc=1,
            device_id={"wide": lax.rem(me_wide + d, wide)},
            device_id_type=MESH,
        )
    for d in range(1, narrow):
        pl.semaphore_signal(
            barrier,
            inc=1,
            device_id={"narrow": lax.rem(me_narrow + d, narrow)},
            device_id_type=MESH,
        )

    with scope("pick"):
        small[0].wait()
        small[1].wait()
        slot_id = lax.broadcasted_iota(jnp.int32, (requests, requests), 0)
        pick = jnp.where(slot_row[...] == slot_id, 1.0, 0.0)
        rows = jnp.dot(
            pick.astype(jnp.bfloat16), hidden[...], preferred_element_type=jnp.float32
        ).astype(jnp.bfloat16)

    def to_owner(block, d):
        row, count = blocks[block]
        peer = lax.rem(me_wide + d, wide)
        return pltpu.make_async_remote_copy(
            src_ref=part.at[peer, pl.ds(row, count)],
            dst_ref=got.at[d - 1, pl.ds(row, count)],
            send_sem=send_sem.at[0],
            recv_sem=recv_sem.at[block],
            device_id={"wide": peer},
            device_id_type=MESH,
        )

    def meets(sent, came, send, recv):
        return pltpu.make_async_remote_copy(
            src_ref=sent,
            dst_ref=came,
            send_sem=send,
            recv_sem=recv,
            device_id={"wide": lax.rem(me_wide + 1, wide)},
            device_id_type=MESH,
        )

    key_rows = key_cols // head_dim * slots
    first_query = 2 * key_rows
    blocks = [(0, 2 * key_rows)] + [
        (first_query + col // head_dim * slots, width // head_dim * slots)
        for col, width in q_blocks
    ]

    def keep(sums, row):
        for t in range(sums.shape[1] // head_dim):
            tile = sums[:, t * head_dim : (t + 1) * head_dim]
            for w in range(wide):
                part[w, row + t * slots : row + (t + 1) * slots] = tile[w * slots : (w + 1) * slots]

    for block, (row, count) in enumerate(blocks):
        if block == 0:
            with scope("kv_in"):
                first[0].wait()
                first[1].wait()
            for copy in stream[ahead : ahead + 2]:
                copy.start()
            with scope("kv_mm"):
                keep(jnp.dot(rows, wk[...], preferred_element_type=jnp.float32), 0)
                keep(jnp.dot(rows, wv[...], preferred_element_type=jnp.float32), key_rows)
            with scope("meet"):
                pl.semaphore_wait(barrier, peers)
        else:
            with scope("q_in%d" % block):
                first[1 + block].wait()
            for copy in stream[ahead + 1 + block : ahead + 2 + block]:
                copy.start()
            if block == len(blocks) - 1:
                for copy in stream[ahead + 2 + block :]:
                    copy.start()
            with scope("q_mm%d" % block):
                col, width = q_blocks[block - 1]
                keep(
                    jnp.dot(rows, wq[:, col : col + width], preferred_element_type=jnp.float32), row
                )
        for d in range(1, wide):
            to_owner(block, d).start()
    with scope("mask"):
        place = lax.broadcasted_iota(jnp.int32, (group, span), 1)
        position = place // kv_local
        kv_of = place - position * kv_local
        scale = 1.0 / jnp.sqrt(jnp.float32(head_dim))
        for copy in small[2:]:
            copy.wait()
        for s in range(slots):
            distance = cycle_offset[s] - position
            distance = jnp.where(distance < 0, distance + window, distance)
            usable = (distance > 0) & (distance < valid_length[s])
            for k in range(kv_local):
                bias[k, s] = jnp.where(usable & (kv_of == k), 0.0, masked_low)

    def summed(block):
        row, count = blocks[block]
        total = part[me_wide, row : row + count]
        if wide > 1:
            rows_in = got.at[:, pl.ds(row, count)]
            meets(rows_in, rows_in, send_sem.at[0], recv_sem.at[block]).wait_recv()
        for d in range(1, wide):
            total = total + got[d - 1, row : row + count]
        return total

    with scope("sum_kv"):
        fresh = summed(0).astype(jnp.bfloat16).astype(jnp.float32)
        keys_fresh = fresh[:key_rows]
        values_fresh = fresh[key_rows:]
        for k in range(kv_local):
            tile = slice(k * head_dim, (k + 1) * head_dim)
            new_keys[:, tile] = keys_fresh[k * slots : (k + 1) * slots].astype(jnp.bfloat16)
            new_values[:, tile] = values_fresh[k * slots : (k + 1) * slots].astype(jnp.bfloat16)

    def to_wide(k, d):
        return pltpu.make_async_remote_copy(
            src_ref=heads_own.at[k],
            dst_ref=heads_got.at[k, d - 1],
            send_sem=send_sem.at[1],
            recv_sem=recv_sem.at[len(blocks) + k],
            device_id={"wide": lax.rem(me_wide + d, wide)},
            device_id_type=MESH,
        )

    for k in range(kv_local):
        with scope("sum_q%d" % k):
            for block in range(1, len(blocks)):
                row, count = blocks[block]
                if q_blocks[block - 1][0] // group_cols == k:
                    queries[row - first_query : row - first_query + count] = summed(block)
        if k == 0:
            with scope("cache_in"):
                for copy in cache_in:
                    copy.wait()
        with scope("attend%d" % k):
            query, scores, weights, own_weight, inverse = [], [], [], [], []
            for s in range(slots):
                query.append(
                    queries[pl.ds(k * group * slots + s, group, stride=slots), :].astype(
                        jnp.bfloat16
                    )
                )
                scores.append(
                    lax.dot_general(
                        query[s],
                        keys[s],
                        (((1,), (1,)), ((), ())),
                        preferred_element_type=jnp.float32,
                    )
                )
            for s in range(slots):
                new_key = keys_fresh[k * slots + s : k * slots + s + 1]
                own_score = (
                    jnp.sum(query[s].astype(jnp.float32) * new_key, axis=1, keepdims=True) * scale
                )
                masked = scores[s] * scale + bias[k, s]
                top = jnp.maximum(jnp.max(masked, axis=1, keepdims=True), own_score)
                spread = jnp.exp(masked - top)
                own = jnp.exp(own_score - top)
                inverse.append(1.0 / (jnp.sum(spread, axis=1, keepdims=True) + own))
                weights.append(spread.astype(jnp.bfloat16))
                own_weight.append(own)
            for s in range(slots):
                new_value = values_fresh[k * slots + s : k * slots + s + 1]
                mixed = jnp.dot(weights[s], values[s], preferred_element_type=jnp.float32)
                heads_own[k, s] = ((mixed + own_weight[s] * new_value) * inverse[s]).astype(
                    jnp.bfloat16
                )
        for d in range(1, wide):
            to_wide(k, d).start()

    held_row = lax.broadcasted_iota(jnp.int32, (requests, requests), 0)
    back = held_row // slots
    held_slot = lax.rem(me_wide - back + wide, wide) * slots + (held_row - back * slots)
    give = jnp.where(slot_row[...] == held_slot, 1.0, 0.0).astype(jnp.bfloat16)

    def gathered(k):
        heads_full[k, 0:slots] = heads_own[k].astype(jnp.float32)
        if wide > 1:
            came = heads_got.at[k]
            meets(came, came, send_sem.at[1], recv_sem.at[len(blocks) + k]).wait_recv()
        for d in range(1, wide):
            heads_full[k, d * slots : (d + 1) * slots] = heads_got[k, d - 1].astype(jnp.float32)
        by_slot = jnp.concatenate(
            [heads_full[k, :, h, :].astype(jnp.bfloat16) for h in range(group)], axis=1
        )
        return lax.dot_general(
            give,
            by_slot,
            (((0,), (0,)), ((), ())),
            preferred_element_type=jnp.float32,
        ).astype(jnp.bfloat16)

    def to_narrow(c, d):
        return pltpu.make_async_remote_copy(
            src_ref=out_part.at[c],
            dst_ref=out_got.at[c, me_narrow],
            send_sem=send_sem.at[2],
            recv_sem=recv_sem.at[len(blocks) + kv_local + c],
            device_id={"narrow": lax.rem(me_narrow + d, narrow)},
            device_id_type=MESH,
        )

    for k in range(kv_local):
        with scope("gather%d" % k):
            heads = gathered(k)
        with scope("out_in%d" % k):
            out_in[k].wait()
        with scope("project%d" % k):
            depth = slice(k * group_cols, (k + 1) * group_cols)
            for c in range(o_chunks):
                cols = slice(c * o_width, (c + 1) * o_width)
                sums = jnp.dot(heads, wo[depth, cols], preferred_element_type=jnp.float32)
                if k > 0:
                    sums = sums + out_early[:, cols]
                if k < kv_local - 1:
                    out_early[:, cols] = sums
                else:
                    out_part[c] = sums.astype(jnp.bfloat16)
                    for d in range(1, narrow):
                        to_narrow(c, d).start()
                    out_got[c, me_narrow] = sums.astype(jnp.bfloat16)
    with scope("total"):
        for c in range(o_chunks):
            cols = slice(c * o_width, (c + 1) * o_width)
            if narrow > 1:
                came = out_got.at[c, pl.ds(0, narrow - 1)]
                meets(
                    came, came, send_sem.at[2], recv_sem.at[len(blocks) + kv_local + c]
                ).wait_recv()
            total = out_got[c, 0].astype(jnp.float32)
            for n in range(1, narrow):
                total = total + out_got[c, n].astype(jnp.float32)
            attn_out[:, cols] = total.astype(jnp.bfloat16)

    with scope("sent"):
        if wide > 1:
            meets(got, got, send_sem.at[0], recv_sem.at[0]).wait_send()
            meets(heads_got, heads_got, send_sem.at[1], recv_sem.at[0]).wait_send()
        if narrow > 1:
            gone = out_got.at[:, pl.ds(0, narrow - 1)]
            meets(gone, gone, send_sem.at[2], recv_sem.at[0]).wait_send()


def finish(attn, keys_new, values_new, attn_out, new_keys, new_values):
    attn_out[...] = attn[...]
    new_keys[...] = keys_new[...]
    new_values[...] = values_new[...]


def per_device(
    wide,
    narrow,
    hidden,
    w_query,
    w_key,
    w_value,
    w_out,
    key_cache,
    value_cache,
    cycle_offset,
    valid_length,
    slot_of,
):
    requests = slot_of.shape[0]
    slots, window, kv_local, head_dim = key_cache.shape
    query_cols = w_query.shape[1]
    key_cols = w_key.shape[1]
    out_cols = w_out.shape[1]
    q_blocks = blocks_of(query_cols, kv_local, wide)
    o_width = width_of(out_cols, o_most)
    q_chunks = len(q_blocks)
    o_chunks = out_cols // o_width
    all_rows = (query_cols + 2 * key_cols) // head_dim * slots
    span = window * kv_local
    vmem = pl.BlockSpec(memory_space=pltpu.VMEM)
    hbm = pl.BlockSpec(memory_space=pltpu.HBM)
    heads_local = query_cols // head_dim
    group = heads_local // kv_local
    outs = (
        jax.ShapeDtypeStruct((requests, out_cols), jnp.bfloat16),
        jax.ShapeDtypeStruct((slots, key_cols), jnp.bfloat16),
        jax.ShapeDtypeStruct((slots, key_cols), jnp.bfloat16),
    )
    results = pl.pallas_call(
        functools.partial(kernel, wide, narrow, kv_local, q_blocks, o_width),
        out_shape=tuple(pltpu.VMEM(out.shape, out.dtype) for out in outs),
        in_specs=[hbm] * 10,
        out_specs=(vmem, vmem, vmem),
        scratch_shapes=[
            pltpu.VMEM(hidden.shape, jnp.bfloat16),
            pltpu.VMEM((1, requests), jnp.int32),
            pltpu.SMEM((slots,), jnp.int32),
            pltpu.SMEM((slots,), jnp.int32),
            pltpu.VMEM(w_query.shape, jnp.bfloat16),
            pltpu.VMEM(w_key.shape, jnp.bfloat16),
            pltpu.VMEM(w_value.shape, jnp.bfloat16),
            pltpu.VMEM(w_out.shape, jnp.bfloat16),
            pltpu.VMEM((slots, span, head_dim), jnp.bfloat16),
            pltpu.VMEM((slots, span, head_dim), jnp.bfloat16),
            pltpu.VMEM((wide, all_rows, head_dim), jnp.float32),
            pltpu.VMEM((wide - 1, all_rows, head_dim), jnp.float32),
            pltpu.VMEM((heads_local * slots, head_dim), jnp.float32),
            pltpu.VMEM((kv_local, slots, group, span), jnp.float32),
            pltpu.VMEM((kv_local, slots, group, head_dim), jnp.bfloat16),
            pltpu.VMEM((kv_local, wide - 1, slots, group, head_dim), jnp.bfloat16),
            pltpu.VMEM((kv_local, wide * slots, group, head_dim), jnp.float32),
            pltpu.VMEM((requests, out_cols), jnp.float32),
            pltpu.VMEM((o_chunks, requests, o_width), jnp.bfloat16),
            pltpu.VMEM((o_chunks, narrow, requests, o_width), jnp.bfloat16),
            pltpu.SemaphoreType.DMA((4 + q_chunks + kv_local,)),
            pltpu.SemaphoreType.DMA((4,)),
            pltpu.SemaphoreType.DMA((3,)),
            pltpu.SemaphoreType.DMA((1 + q_chunks + kv_local + o_chunks,)),
        ],
        compiler_params=pltpu.CompilerParams(
            collective_id=0, has_side_effects=True, vmem_limit_bytes=main_kib * 1024
        ),
        name="decode_step",
    )(
        hidden,
        w_query,
        w_key,
        w_value,
        w_out,
        key_cache.reshape(slots, span, head_dim),
        value_cache.reshape(slots, span, head_dim),
        slot_of.reshape(1, requests),
        cycle_offset,
        valid_length,
    )
    return pl.pallas_call(
        finish,
        out_shape=outs,
        in_specs=[vmem] * 3,
        out_specs=(vmem,) * 3,
        compiler_params=pltpu.CompilerParams(vmem_limit_bytes=finish_kib * 1024),
        name="finish",
    )(*results)


def solution(mesh):
    placed = (
        P("groups", "wide"),
        P("wide", "narrow"),
        P("wide", "narrow"),
        P("wide", "narrow"),
        P("narrow", "wide"),
        P(("groups", "wide"), None, "narrow", None),
        P(("groups", "wide"), None, "narrow", None),
        P(("groups", "wide")),
        P(("groups", "wide")),
        P("groups"),
    )
    return jax.shard_map(
        functools.partial(per_device, mesh.shape["wide"], mesh.shape["narrow"]),
        mesh=mesh,
        in_specs=placed,
        out_specs=(
            P("groups", "wide"),
            P(("groups", "wide"), "narrow"),
            P(("groups", "wide"), "narrow"),
        ),
        check_vma=False,
    )
```

```python
import functools

import jax
import jax.numpy as jnp
from jax import lax
from jax.experimental import pallas as pl
from jax.experimental.pallas import tpu as pltpu
from jax.sharding import PartitionSpec as P

masked_low = -1e30
scope = jax.named_scope
MESH = pl.DeviceIdType.MESH
head_parts = 2
finish_kib = 1024
main_kib = 64512
o_most = 1024
ahead = 4
meet_after = 0


def width_of(columns, most):
    width = min(columns, most)
    while columns % width:
        width -= 128
    return width


def blocks_of(columns, kv_local, wide):
    per_head = columns // kv_local
    parts = head_parts if wide <= 8 else 1
    width = width_of(per_head, max(per_head // parts // 128 * 128, 128))
    return tuple((col, width) for col in range(0, columns, width))


def kernel(
    wide,
    narrow,
    kv_local,
    q_blocks,
    o_width,
    hidden_in,
    w_query,
    w_key,
    w_value,
    w_out,
    key_cache,
    value_cache,
    slot_row_in,
    cycle_offset_in,
    valid_length_in,
    attn_out,
    new_keys,
    new_values,
    hidden,
    slot_row,
    cycle_offset,
    valid_length,
    wq,
    wk,
    wv,
    wo,
    keys,
    values,
    keys_across,
    kv_part,
    kv_got,
    q_own,
    q_part,
    q_got,
    queries,
    bias,
    heads_own,
    heads_got,
    heads_full,
    out_early,
    out_part,
    out_got,
    in_sem,
    small_sem,
    send_sem,
    recv_sem,
):
    me_wide = lax.axis_index("wide")
    me_narrow = lax.axis_index("narrow")
    requests = hidden.shape[0]
    slots = keys.shape[0]
    head_dim = keys.shape[2]
    span = keys.shape[1]
    window = span // kv_local
    query_cols = wq.shape[1]
    key_cols = wk.shape[1]
    out_cols = wo.shape[1]
    heads_local = query_cols // head_dim
    group = heads_local // kv_local
    group_cols = group * head_dim
    q_chunks = len(q_blocks)
    o_chunks = out_cols // o_width

    first = [
        pltpu.make_async_copy(w_key, wk, in_sem.at[0]),
        pltpu.make_async_copy(w_value, wv, in_sem.at[1]),
    ]
    depth = wq.shape[0]
    pieces = [(col, width, 0, depth) for col, width in q_blocks]
    col, width = q_blocks[-1]
    half = depth // 32 * 16
    pieces[-1:] = [(col, width, 0, half), (col, width, half, depth - half)]
    for c, (col, width, row, count) in enumerate(pieces):
        part = (pl.ds(row, count), pl.ds(col, width))
        first.append(pltpu.make_async_copy(w_query.at[part], wq.at[part], in_sem.at[2 + c]))
    base = 2 + len(pieces)
    cache_in = [
        pltpu.make_async_copy(key_cache, keys, in_sem.at[base]),
        pltpu.make_async_copy(value_cache, values, in_sem.at[base + 1]),
    ]
    out_in = []
    for k in range(kv_local):
        span_k = pl.ds(k * group_cols, group_cols)
        out_in.append(
            pltpu.make_async_copy(w_out.at[span_k], wo.at[span_k], in_sem.at[base + 2 + k])
        )
    small = [
        pltpu.make_async_copy(hidden_in, hidden, small_sem.at[0]),
        pltpu.make_async_copy(slot_row_in, slot_row, small_sem.at[1]),
        pltpu.make_async_copy(cycle_offset_in, cycle_offset, small_sem.at[2]),
        pltpu.make_async_copy(valid_length_in, valid_length, small_sem.at[3]),
    ]
    stream = first + cache_in + out_in
    for copy in small[:2] + stream[:ahead] + small[2:]:
        copy.start()
    del stream[:ahead]

    barrier = pltpu.get_barrier_semaphore()
    peers = wide + narrow - 2
    for d in range(1, wide):
        pl.semaphore_signal(
            barrier,
            inc=1,
            device_id={"wide": lax.rem(me_wide + d, wide)},
            device_id_type=MESH,
        )
    for d in range(1, narrow):
        pl.semaphore_signal(
            barrier,
            inc=1,
            device_id={"narrow": lax.rem(me_narrow + d, narrow)},
            device_id_type=MESH,
        )

    with scope("pick"):
        small[0].wait()
        small[1].wait()
        slot_id = lax.broadcasted_iota(jnp.int32, (requests, requests), 0)
        pick = jnp.where(slot_row[...] == slot_id, 1.0, 0.0)
        rows = jnp.dot(
            pick.astype(jnp.bfloat16), hidden[...], preferred_element_type=jnp.float32
        ).astype(jnp.bfloat16)

    def to_owner(block, d):
        peer = lax.rem(me_wide + d, wide)
        part, got = (
            (kv_part, kv_got) if block == 0 else (q_part.at[block - 1], q_got.at[block - 1])
        )
        return pltpu.make_async_remote_copy(
            src_ref=part.at[peer],
            dst_ref=got.at[d - 1],
            send_sem=send_sem.at[min(block, 1)],
            recv_sem=recv_sem.at[block],
            device_id={"wide": peer},
            device_id_type=MESH,
        )

    def meets(sent, came, send, recv):
        return pltpu.make_async_remote_copy(
            src_ref=sent,
            dst_ref=came,
            send_sem=send,
            recv_sem=recv,
            device_id={"wide": lax.rem(me_wide + 1, wide)},
            device_id_type=MESH,
        )

    def by_owner(sums):
        return sums.reshape(wide, slots, sums.shape[1])

    def send(block):
        for d in range(1, wide):
            to_owner(block, d).start()

    def go(count):
        for _ in range(min(count, len(stream))):
            stream.pop(0).start()

    with scope("kv_in"):
        first[0].wait()
        first[1].wait()
    go(len(first) - ahead)
    with scope("kv_mm"):
        sums = jnp.dot(rows, wk[...], preferred_element_type=jnp.float32)
        kv_part[:, :, :key_cols] = by_owner(sums)
        sums = jnp.dot(rows, wv[...], preferred_element_type=jnp.float32)
        kv_part[:, :, key_cols:] = by_owner(sums)
    ready = [0]
    for c, (col, width, row, count) in enumerate(pieces):
        with scope("q_in%d" % c):
            first[2 + c].wait()
        if c >= len(pieces) - 3:
            go(1)
        with scope("q_mm%d" % c):
            sums = jnp.dot(
                rows[:, row : row + count],
                wq[row : row + count, col : col + width],
                preferred_element_type=jnp.float32,
            )
            if row > 0:
                sums = sums + early
            early = sums
            block = col // width
            if row + count == depth:
                q_own[block] = by_owner(sums)
                q_part[block] = by_owner(sums).astype(jnp.bfloat16)
        if row + count == depth:
            ready.append(1 + block)
        if c == min(meet_after, len(pieces) - 1):
            with scope("meet"):
                pl.semaphore_wait(barrier, peers)
        if c >= min(meet_after, len(pieces) - 1):
            while ready:
                send(ready.pop(0))
    go(len(stream))

    with scope("mask"):
        place = lax.broadcasted_iota(jnp.int32, (group, span), 1)
        position = place // kv_local
        kv_of = place - position * kv_local
        scale = 1.0 / jnp.sqrt(jnp.float32(head_dim))
        for copy in small[2:]:
            copy.wait()
        for s in range(slots):
            distance = cycle_offset[s] - position
            distance = jnp.where(distance < 0, distance + window, distance)
            usable = (distance > 0) & (distance < valid_length[s])
            for k in range(kv_local):
                bias[k, s] = jnp.where(usable & (kv_of == k), 0.0, masked_low)

    with scope("keys_in"):
        cache_in[0].wait()
    with scope("turn"):
        for s in range(slots):
            keys_across[s] = keys[s].T

    def summed(block):
        own, got = (kv_part, kv_got) if block == 0 else (q_own.at[block - 1], q_got.at[block - 1])
        total = own[me_wide]
        if wide > 1:
            meets(got, got, send_sem.at[0], recv_sem.at[block]).wait_recv()
        for d in range(1, wide):
            total = total + got[d - 1].astype(jnp.float32)
        return total

    with scope("sum_kv"):
        fresh = summed(0).astype(jnp.bfloat16)
        new_keys[...] = fresh[:, :key_cols]
        new_values[...] = fresh[:, key_cols:]
        fresh = fresh.astype(jnp.float32)

    def to_wide(k, d):
        return pltpu.make_async_remote_copy(
            src_ref=heads_own.at[k],
            dst_ref=heads_got.at[k, d - 1],
            send_sem=send_sem.at[2],
            recv_sem=recv_sem.at[1 + q_chunks + k],
            device_id={"wide": lax.rem(me_wide + d, wide)},
            device_id_type=MESH,
        )

    for k in range(kv_local):
        with scope("sum_q%d" % k):
            for block, (col, width) in enumerate(q_blocks, 1):
                if col // group_cols == k:
                    sums = summed(block)
                    for t in range(width // head_dim):
                        row = (col // head_dim + t) * slots
                        queries[row : row + slots] = sums[:, t * head_dim : (t + 1) * head_dim]
        if k == 0:
            with scope("values_in"):
                cache_in[1].wait()
        with scope("attend%d" % k):
            query, scores, weights, own_weight, inverse = [], [], [], [], []
            for s in range(slots):
                query.append(
                    queries[pl.ds(k * group * slots + s, group, stride=slots), :].astype(
                        jnp.bfloat16
                    )
                )
                scores.append(
                    jnp.dot(query[s], keys_across[s], preferred_element_type=jnp.float32)
                )
            for s in range(slots):
                new_key = fresh[s : s + 1, k * head_dim : (k + 1) * head_dim]
                own_score = (
                    jnp.sum(query[s].astype(jnp.float32) * new_key, axis=1, keepdims=True) * scale
                )
                masked = scores[s] * scale + bias[k, s]
                top = jnp.maximum(jnp.max(masked, axis=1, keepdims=True), own_score)
                spread = jnp.exp(masked - top)
                own = jnp.exp(own_score - top)
                inverse.append(1.0 / (jnp.sum(spread, axis=1, keepdims=True) + own))
                weights.append(spread.astype(jnp.bfloat16))
                own_weight.append(own)
            for s in range(slots):
                col = key_cols + k * head_dim
                new_value = fresh[s : s + 1, col : col + head_dim]
                mixed = jnp.dot(weights[s], values[s], preferred_element_type=jnp.float32)
                heads_own[k, s] = ((mixed + own_weight[s] * new_value) * inverse[s]).astype(
                    jnp.bfloat16
                )
        for d in range(1, wide):
            to_wide(k, d).start()

    held_row = lax.broadcasted_iota(jnp.int32, (requests, requests), 0)
    back = held_row // slots
    held_slot = lax.rem(me_wide - back + wide, wide) * slots + (held_row - back * slots)
    give = jnp.where(slot_row[...] == held_slot, 1.0, 0.0).astype(jnp.bfloat16)

    def gathered(k):
        heads_full[k, 0:slots] = heads_own[k].astype(jnp.float32)
        if wide > 1:
            came = heads_got.at[k]
            meets(came, came, send_sem.at[2], recv_sem.at[1 + q_chunks + k]).wait_recv()
        for d in range(1, wide):
            heads_full[k, d * slots : (d + 1) * slots] = heads_got[k, d - 1].astype(jnp.float32)
        by_slot = jnp.concatenate(
            [heads_full[k, :, h, :].astype(jnp.bfloat16) for h in range(group)], axis=1
        )
        return lax.dot_general(
            give,
            by_slot,
            (((0,), (0,)), ((), ())),
            preferred_element_type=jnp.float32,
        ).astype(jnp.bfloat16)

    if narrow == 4:
        others = [
            lax.rem(me_narrow + 2, 4),
            3 - me_narrow,
            me_narrow + 1 - 2 * lax.rem(me_narrow, 2),
        ]
    else:
        others = [lax.rem(me_narrow + d, narrow) for d in range(1, narrow)]

    def to_narrow(c, peer):
        return pltpu.make_async_remote_copy(
            src_ref=out_part.at[c],
            dst_ref=out_got.at[c, me_narrow],
            send_sem=send_sem.at[3],
            recv_sem=recv_sem.at[1 + q_chunks + kv_local + c],
            device_id={"narrow": peer},
            device_id_type=MESH,
        )

    for k in range(kv_local):
        with scope("gather%d" % k):
            heads = gathered(k)
        with scope("out_in%d" % k):
            out_in[k].wait()
        with scope("project%d" % k):
            span_k = slice(k * group_cols, (k + 1) * group_cols)
            for c in range(o_chunks):
                cols = slice(c * o_width, (c + 1) * o_width)
                sums = jnp.dot(heads, wo[span_k, cols], preferred_element_type=jnp.float32)
                if k > 0:
                    sums = sums + out_early[:, cols]
                if k < kv_local - 1:
                    out_early[:, cols] = sums
                else:
                    out_part[c] = sums.astype(jnp.bfloat16)
                    for peer in others[:1]:
                        to_narrow(c, peer).start()
                    if c > 0:
                        for peer in others[1:]:
                            to_narrow(c - 1, peer).start()
                    if c == o_chunks - 1:
                        for peer in others[1:]:
                            to_narrow(c, peer).start()
                    out_got[c, me_narrow] = sums.astype(jnp.bfloat16)
    with scope("total"):
        for c in range(o_chunks):
            cols = slice(c * o_width, (c + 1) * o_width)
            if narrow > 1:
                came = out_got.at[c, pl.ds(0, narrow - 1)]
                meets(
                    came, came, send_sem.at[3], recv_sem.at[1 + q_chunks + kv_local + c]
                ).wait_recv()
            total = out_got[c, 0].astype(jnp.float32)
            for n in range(1, narrow):
                total = total + out_got[c, n].astype(jnp.float32)
            attn_out[:, cols] = total.astype(jnp.bfloat16)

    with scope("sent"):
        if wide > 1:
            meets(kv_got, kv_got, send_sem.at[0], recv_sem.at[0]).wait_send()
            meets(q_got, q_got, send_sem.at[1], recv_sem.at[0]).wait_send()
            meets(heads_got, heads_got, send_sem.at[2], recv_sem.at[0]).wait_send()
        if narrow > 1:
            gone = out_got.at[:, pl.ds(0, narrow - 1)]
            meets(gone, gone, send_sem.at[3], recv_sem.at[0]).wait_send()


def finish(attn, keys_new, values_new, attn_out, new_keys, new_values):
    attn_out[...] = attn[...]
    new_keys[...] = keys_new[...]
    new_values[...] = values_new[...]


def per_device(
    wide,
    narrow,
    hidden,
    w_query,
    w_key,
    w_value,
    w_out,
    key_cache,
    value_cache,
    cycle_offset,
    valid_length,
    slot_of,
):
    requests = slot_of.shape[0]
    slots, window, kv_local, head_dim = key_cache.shape
    query_cols = w_query.shape[1]
    key_cols = w_key.shape[1]
    out_cols = w_out.shape[1]
    q_blocks = blocks_of(query_cols, kv_local, wide)
    o_width = width_of(out_cols, o_most)
    q_chunks = len(q_blocks)
    o_chunks = out_cols // o_width
    q_width = q_blocks[0][1]
    span = window * kv_local
    vmem = pl.BlockSpec(memory_space=pltpu.VMEM)
    hbm = pl.BlockSpec(memory_space=pltpu.HBM)
    heads_local = query_cols // head_dim
    group = heads_local // kv_local
    outs = (
        jax.ShapeDtypeStruct((requests, out_cols), jnp.bfloat16),
        jax.ShapeDtypeStruct((slots, key_cols), jnp.bfloat16),
        jax.ShapeDtypeStruct((slots, key_cols), jnp.bfloat16),
    )
    results = pl.pallas_call(
        functools.partial(kernel, wide, narrow, kv_local, q_blocks, o_width),
        out_shape=tuple(pltpu.VMEM(out.shape, out.dtype) for out in outs),
        in_specs=[hbm] * 10,
        out_specs=(vmem, vmem, vmem),
        scratch_shapes=[
            pltpu.VMEM(hidden.shape, jnp.bfloat16),
            pltpu.VMEM((1, requests), jnp.int32),
            pltpu.SMEM((slots,), jnp.int32),
            pltpu.SMEM((slots,), jnp.int32),
            pltpu.VMEM(w_query.shape, jnp.bfloat16),
            pltpu.VMEM(w_key.shape, jnp.bfloat16),
            pltpu.VMEM(w_value.shape, jnp.bfloat16),
            pltpu.VMEM(w_out.shape, jnp.bfloat16),
            pltpu.VMEM((slots, span, head_dim), jnp.bfloat16),
            pltpu.VMEM((slots, span, head_dim), jnp.bfloat16),
            pltpu.VMEM((slots, head_dim, span), jnp.bfloat16),
            pltpu.VMEM((wide, slots, 2 * key_cols), jnp.float32),
            pltpu.VMEM((wide - 1, slots, 2 * key_cols), jnp.float32),
            pltpu.VMEM((q_chunks, wide, slots, q_width), jnp.float32),
            pltpu.VMEM((q_chunks, wide, slots, q_width), jnp.bfloat16),
            pltpu.VMEM((q_chunks, wide - 1, slots, q_width), jnp.bfloat16),
            pltpu.VMEM((heads_local * slots, head_dim), jnp.float32),
            pltpu.VMEM((kv_local, slots, group, span), jnp.float32),
            pltpu.VMEM((kv_local, slots, group, head_dim), jnp.bfloat16),
            pltpu.VMEM((kv_local, wide - 1, slots, group, head_dim), jnp.bfloat16),
            pltpu.VMEM((kv_local, wide * slots, group, head_dim), jnp.float32),
            pltpu.VMEM((requests, out_cols), jnp.float32),
            pltpu.VMEM((o_chunks, requests, o_width), jnp.bfloat16),
            pltpu.VMEM((o_chunks, narrow, requests, o_width), jnp.bfloat16),
            pltpu.SemaphoreType.DMA((5 + q_chunks + kv_local,)),
            pltpu.SemaphoreType.DMA((4,)),
            pltpu.SemaphoreType.DMA((4,)),
            pltpu.SemaphoreType.DMA((1 + q_chunks + kv_local + o_chunks,)),
        ],
        compiler_params=pltpu.CompilerParams(
            collective_id=0, has_side_effects=True, vmem_limit_bytes=main_kib * 1024
        ),
        name="decode_step",
    )(
        hidden,
        w_query,
        w_key,
        w_value,
        w_out,
        key_cache.reshape(slots, span, head_dim),
        value_cache.reshape(slots, span, head_dim),
        slot_of.reshape(1, requests),
        cycle_offset,
        valid_length,
    )
    return pl.pallas_call(
        finish,
        out_shape=outs,
        in_specs=[vmem] * 3,
        out_specs=(vmem,) * 3,
        compiler_params=pltpu.CompilerParams(vmem_limit_bytes=finish_kib * 1024),
        name="finish",
    )(*results)


def solution(mesh):
    placed = (
        P("groups", "wide"),
        P("wide", "narrow"),
        P("wide", "narrow"),
        P("wide", "narrow"),
        P("narrow", "wide"),
        P(("groups", "wide"), None, "narrow", None),
        P(("groups", "wide"), None, "narrow", None),
        P(("groups", "wide")),
        P(("groups", "wide")),
        P("groups"),
    )
    return jax.shard_map(
        functools.partial(per_device, mesh.shape["wide"], mesh.shape["narrow"]),
        mesh=mesh,
        in_specs=placed,
        out_specs=(
            P("groups", "wide"),
            P(("groups", "wide"), "narrow"),
            P(("groups", "wide"), "narrow"),
        ),
        check_vma=False,
    )
```

```python
import functools

import jax
import jax.numpy as jnp
from jax import lax
from jax.experimental import pallas as pl
from jax.experimental.pallas import tpu as pltpu
from jax.sharding import PartitionSpec as P

masked_low = -1e30
scope = jax.named_scope
MESH = pl.DeviceIdType.MESH
head_parts = 2
finish_kib = 1024
main_kib = 64512
o_most = 512
ahead = 4
meet_after = 0


def width_of(columns, most):
    width = min(columns, most)
    while columns % width:
        width -= 128
    return width


def blocks_of(columns, kv_local, wide):
    per_head = columns // kv_local
    parts = head_parts if wide <= 8 else 1
    width = width_of(per_head, max(per_head // parts // 128 * 128, 128))
    return tuple((col, width) for col in range(0, columns, width))


def kernel(
    wide,
    narrow,
    kv_local,
    q_blocks,
    o_width,
    hidden_in,
    w_query,
    w_key,
    w_value,
    w_out,
    key_cache,
    value_cache,
    slot_row_in,
    cycle_offset_in,
    valid_length_in,
    attn_out,
    new_keys,
    new_values,
    hidden,
    slot_row,
    cycle_offset,
    valid_length,
    wq,
    wk,
    wv,
    wo,
    keys,
    values,
    keys_across,
    kv_part,
    kv_got,
    q_own,
    q_part,
    q_got,
    queries,
    bias,
    heads_own,
    heads_got,
    heads_made,
    out_early,
    out_part,
    out_got,
    in_sem,
    small_sem,
    send_sem,
    recv_sem,
):
    me_wide = lax.axis_index("wide")
    me_narrow = lax.axis_index("narrow")
    requests = hidden.shape[0]
    slots = keys.shape[0]
    head_dim = keys.shape[2]
    span = keys.shape[1]
    window = span // kv_local
    query_cols = wq.shape[1]
    key_cols = wk.shape[1]
    out_cols = wo.shape[1]
    heads_local = query_cols // head_dim
    group = heads_local // kv_local
    group_cols = group * head_dim
    q_chunks = len(q_blocks)
    o_chunks = out_cols // o_width

    first = [
        pltpu.make_async_copy(w_key, wk, in_sem.at[0]),
        pltpu.make_async_copy(w_value, wv, in_sem.at[1]),
    ]
    depth = wq.shape[0]
    pieces = [(col, width, 0, depth) for col, width in q_blocks]
    col, width = q_blocks[-1]
    half = depth // 32 * 16
    pieces[-1:] = [(col, width, 0, half), (col, width, half, depth - half)]
    for c, (col, width, row, count) in enumerate(pieces):
        part = (pl.ds(row, count), pl.ds(col, width))
        first.append(pltpu.make_async_copy(w_query.at[part], wq.at[part], in_sem.at[2 + c]))
    base = 2 + len(pieces)
    cache_in = [
        pltpu.make_async_copy(key_cache, keys, in_sem.at[base]),
        pltpu.make_async_copy(value_cache, values, in_sem.at[base + 1]),
    ]
    out_in = []
    for k in range(kv_local):
        span_k = pl.ds(k * group_cols, group_cols)
        out_in.append(
            pltpu.make_async_copy(w_out.at[span_k], wo.at[span_k], in_sem.at[base + 2 + k])
        )
    small = [
        pltpu.make_async_copy(hidden_in, hidden, small_sem.at[0]),
        pltpu.make_async_copy(slot_row_in, slot_row, small_sem.at[1]),
        pltpu.make_async_copy(cycle_offset_in, cycle_offset, small_sem.at[2]),
        pltpu.make_async_copy(valid_length_in, valid_length, small_sem.at[3]),
    ]
    stream = first + cache_in + out_in
    for copy in small[:2] + stream[:ahead] + small[2:]:
        copy.start()
    del stream[:ahead]

    barrier = pltpu.get_barrier_semaphore()
    peers = wide + narrow - 2
    for d in range(1, wide):
        pl.semaphore_signal(
            barrier,
            inc=1,
            device_id={"wide": lax.rem(me_wide + d, wide)},
            device_id_type=MESH,
        )
    for d in range(1, narrow):
        pl.semaphore_signal(
            barrier,
            inc=1,
            device_id={"narrow": lax.rem(me_narrow + d, narrow)},
            device_id_type=MESH,
        )

    with scope("pick"):
        small[0].wait()
        small[1].wait()
        slot_id = lax.broadcasted_iota(jnp.int32, (requests, requests), 0)
        pick = jnp.where(slot_row[...] == slot_id, 1.0, 0.0)
        rows = jnp.dot(
            pick.astype(jnp.bfloat16), hidden[...], preferred_element_type=jnp.float32
        ).astype(jnp.bfloat16)

    def to_owner(block, d):
        peer = lax.rem(me_wide + d, wide)
        part, got = (
            (kv_part, kv_got) if block == 0 else (q_part.at[block - 1], q_got.at[block - 1])
        )
        return pltpu.make_async_remote_copy(
            src_ref=part.at[peer],
            dst_ref=got.at[d - 1],
            send_sem=send_sem.at[min(block, 1)],
            recv_sem=recv_sem.at[block],
            device_id={"wide": peer},
            device_id_type=MESH,
        )

    def meets(sent, came, send, recv):
        return pltpu.make_async_remote_copy(
            src_ref=sent,
            dst_ref=came,
            send_sem=send,
            recv_sem=recv,
            device_id={"wide": lax.rem(me_wide + 1, wide)},
            device_id_type=MESH,
        )

    def by_owner(sums):
        return sums.reshape(wide, slots, sums.shape[1])

    def send(block):
        for d in range(1, wide):
            to_owner(block, d).start()

    def go(count):
        for _ in range(min(count, len(stream))):
            stream.pop(0).start()

    with scope("kv_in"):
        first[0].wait()
        first[1].wait()
    go(len(first) - ahead)
    with scope("kv_mm"):
        sums = jnp.dot(rows, wk[...], preferred_element_type=jnp.float32)
        kv_part[:, :, :key_cols] = by_owner(sums)
        sums = jnp.dot(rows, wv[...], preferred_element_type=jnp.float32)
        kv_part[:, :, key_cols:] = by_owner(sums)
    ready = [0]
    for c, (col, width, row, count) in enumerate(pieces):
        with scope("q_in%d" % c):
            first[2 + c].wait()
        if c >= len(pieces) - 3:
            go(1)
        with scope("q_mm%d" % c):
            sums = jnp.dot(
                rows[:, row : row + count],
                wq[row : row + count, col : col + width],
                preferred_element_type=jnp.float32,
            )
            if row > 0:
                sums = sums + early
            early = sums
            block = col // width
            if row + count == depth:
                q_part[block] = by_owner(sums).astype(jnp.bfloat16)
        if row + count == depth:
            ready.append(1 + block)
        if c == min(meet_after, len(pieces) - 1):
            with scope("meet"):
                pl.semaphore_wait(barrier, peers)
        if c >= min(meet_after, len(pieces) - 1):
            while ready:
                send(ready.pop(0))
        if row + count == depth:
            q_own[block] = by_owner(sums)
    go(len(stream))

    with scope("mask"):
        place = lax.broadcasted_iota(jnp.int32, (group, span), 1)
        position = place // kv_local
        kv_of = place - position * kv_local
        scale = 1.0 / jnp.sqrt(jnp.float32(head_dim))
        for copy in small[2:]:
            copy.wait()
        for s in range(slots):
            distance = cycle_offset[s] - position
            distance = jnp.where(distance < 0, distance + window, distance)
            usable = (distance > 0) & (distance < valid_length[s])
            for k in range(kv_local):
                bias[k, s] = jnp.where(usable & (kv_of == k), 0.0, masked_low)

    with scope("keys_in"):
        cache_in[0].wait()
    with scope("turn"):
        for s in range(slots):
            keys_across[s] = keys[s].T

    def summed(block):
        own, got = (kv_part, kv_got) if block == 0 else (q_own.at[block - 1], q_got.at[block - 1])
        total = own[me_wide]
        if wide > 1:
            meets(got, got, send_sem.at[0], recv_sem.at[block]).wait_recv()
        for d in range(1, wide):
            total = total + got[d - 1].astype(jnp.float32)
        return total

    with scope("sum_kv"):
        fresh = summed(0).astype(jnp.bfloat16)
        new_keys[...] = fresh[:, :key_cols]
        new_values[...] = fresh[:, key_cols:]
        fresh = fresh.astype(jnp.float32)

    def to_wide(k, i):
        peer = i + (i - me_wide + wide) // wide
        back = lax.rem(peer - me_wide + wide, wide)
        return pltpu.make_async_remote_copy(
            src_ref=heads_own.at[k],
            dst_ref=heads_got.at[k, back - 1],
            send_sem=send_sem.at[2],
            recv_sem=recv_sem.at[1 + q_chunks + k],
            device_id={"wide": peer},
            device_id_type=MESH,
        )

    for k in range(kv_local):
        with scope("sum_q%d" % k):
            for block, (col, width) in enumerate(q_blocks, 1):
                if col // group_cols == k:
                    sums = summed(block)
                    for t in range(width // head_dim):
                        row = (col // head_dim + t) * slots
                        queries[row : row + slots] = sums[:, t * head_dim : (t + 1) * head_dim]
        if k == 0:
            with scope("values_in"):
                cache_in[1].wait()
        with scope("attend%d" % k):
            query, scores, weights, own_weight, inverse = [], [], [], [], []
            for s in range(slots):
                query.append(
                    queries[pl.ds(k * group * slots + s, group, stride=slots), :].astype(
                        jnp.bfloat16
                    )
                )
                scores.append(
                    jnp.dot(query[s], keys_across[s], preferred_element_type=jnp.float32)
                )
            for s in range(slots):
                new_key = fresh[s : s + 1, k * head_dim : (k + 1) * head_dim]
                own_score = (
                    jnp.sum(query[s].astype(jnp.float32) * new_key, axis=1, keepdims=True) * scale
                )
                masked = scores[s] * scale + bias[k, s]
                top = jnp.maximum(jnp.max(masked, axis=1, keepdims=True), own_score)
                spread = jnp.exp(masked - top)
                own = jnp.exp(own_score - top)
                inverse.append(1.0 / (jnp.sum(spread, axis=1, keepdims=True) + own))
                weights.append(spread.astype(jnp.bfloat16))
                own_weight.append(own)
            for s in range(slots):
                col = key_cols + k * head_dim
                new_value = fresh[s : s + 1, col : col + head_dim]
                mixed = jnp.dot(weights[s], values[s], preferred_element_type=jnp.float32)
                heads_made[s] = (mixed + own_weight[s] * new_value) * inverse[s]
            heads_own[k] = jnp.concatenate(
                [heads_made[:, h, :] for h in range(group)], axis=1
            ).astype(jnp.bfloat16)
        for i in range(wide - 1):
            to_wide(k, i).start()

    held_row = lax.broadcasted_iota(jnp.int32, (requests, requests), 0)
    back = held_row // slots
    held_slot = lax.rem(me_wide - back + wide, wide) * slots + (held_row - back * slots)
    give = jnp.where(slot_row[...] == held_slot, 1.0, 0.0).astype(jnp.bfloat16)

    def gathered(k):
        if wide > 1:
            came = heads_got.at[k]
            meets(came, came, send_sem.at[2], recv_sem.at[1 + q_chunks + k]).wait_recv()
        by_slot = jnp.concatenate(
            [heads_own[k].astype(jnp.float32)]
            + [heads_got[k, d - 1].astype(jnp.float32) for d in range(1, wide)],
            axis=0,
        ).astype(jnp.bfloat16)
        return lax.dot_general(
            give,
            by_slot,
            (((0,), (0,)), ((), ())),
            preferred_element_type=jnp.float32,
        ).astype(jnp.bfloat16)

    if narrow == 4:
        others = [
            lax.rem(me_narrow + 2, 4),
            3 - me_narrow,
            me_narrow + 1 - 2 * lax.rem(me_narrow, 2),
        ]
    else:
        others = [lax.rem(me_narrow + d, narrow) for d in range(1, narrow)]

    def to_narrow(c, peer):
        return pltpu.make_async_remote_copy(
            src_ref=out_part.at[c],
            dst_ref=out_got.at[c, me_narrow],
            send_sem=send_sem.at[3],
            recv_sem=recv_sem.at[1 + q_chunks + kv_local + c],
            device_id={"narrow": peer},
            device_id_type=MESH,
        )

    for k in range(kv_local):
        with scope("gather%d" % k):
            heads = gathered(k)
        with scope("out_in%d" % k):
            out_in[k].wait()
        with scope("project%d" % k):
            span_k = slice(k * group_cols, (k + 1) * group_cols)

            def product(c):
                cols = slice(c * o_width, (c + 1) * o_width)
                sums = jnp.dot(heads, wo[span_k, cols], preferred_element_type=jnp.float32)
                return sums + out_early[:, cols] if k > 0 else sums

            if k < kv_local - 1:
                for c in range(o_chunks):
                    out_early[:, c * o_width : (c + 1) * o_width] = product(c)
            else:
                after = product(0)
                for c in range(o_chunks):
                    sums = after
                    if c + 1 < o_chunks:
                        after = product(c + 1)
                    out_part[c] = sums.astype(jnp.bfloat16)
                    out_got[c, me_narrow] = sums.astype(jnp.bfloat16)
                    for peer in others[:1]:
                        to_narrow(c, peer).start()
                for peer in others[1:]:
                    for c in range(o_chunks):
                        to_narrow(c, peer).start()
    with scope("total"):
        for c in range(o_chunks):
            cols = slice(c * o_width, (c + 1) * o_width)
            if narrow > 1:
                came = out_got.at[c, pl.ds(0, narrow - 1)]
                meets(
                    came, came, send_sem.at[3], recv_sem.at[1 + q_chunks + kv_local + c]
                ).wait_recv()
            total = out_got[c, 0].astype(jnp.float32)
            for n in range(1, narrow):
                total = total + out_got[c, n].astype(jnp.float32)
            attn_out[:, cols] = total.astype(jnp.bfloat16)

    with scope("sent"):
        if wide > 1:
            meets(kv_got, kv_got, send_sem.at[0], recv_sem.at[0]).wait_send()
            meets(q_got, q_got, send_sem.at[1], recv_sem.at[0]).wait_send()
            meets(heads_got, heads_got, send_sem.at[2], recv_sem.at[0]).wait_send()
        if narrow > 1:
            gone = out_got.at[:, pl.ds(0, narrow - 1)]
            meets(gone, gone, send_sem.at[3], recv_sem.at[0]).wait_send()


def finish(attn, keys_new, values_new, attn_out, new_keys, new_values, sem):
    copies = [
        pltpu.make_async_copy(attn, attn_out, sem.at[0]),
        pltpu.make_async_copy(keys_new, new_keys, sem.at[1]),
        pltpu.make_async_copy(values_new, new_values, sem.at[2]),
    ]
    for copy in copies:
        copy.start()
    for copy in copies:
        copy.wait()


def per_device(
    wide,
    narrow,
    hidden,
    w_query,
    w_key,
    w_value,
    w_out,
    key_cache,
    value_cache,
    cycle_offset,
    valid_length,
    slot_of,
):
    requests = slot_of.shape[0]
    slots, window, kv_local, head_dim = key_cache.shape
    query_cols = w_query.shape[1]
    key_cols = w_key.shape[1]
    out_cols = w_out.shape[1]
    q_blocks = blocks_of(query_cols, kv_local, wide)
    o_width = width_of(out_cols, o_most)
    q_chunks = len(q_blocks)
    o_chunks = out_cols // o_width
    q_width = q_blocks[0][1]
    span = window * kv_local
    vmem = pl.BlockSpec(memory_space=pltpu.VMEM)
    hbm = pl.BlockSpec(memory_space=pltpu.HBM)
    heads_local = query_cols // head_dim
    group = heads_local // kv_local
    outs = (
        jax.ShapeDtypeStruct((requests, out_cols), jnp.bfloat16),
        jax.ShapeDtypeStruct((slots, key_cols), jnp.bfloat16),
        jax.ShapeDtypeStruct((slots, key_cols), jnp.bfloat16),
    )
    results = pl.pallas_call(
        functools.partial(kernel, wide, narrow, kv_local, q_blocks, o_width),
        out_shape=tuple(pltpu.VMEM(out.shape, out.dtype) for out in outs),
        in_specs=[hbm] * 10,
        out_specs=(vmem, vmem, vmem),
        scratch_shapes=[
            pltpu.VMEM(hidden.shape, jnp.bfloat16),
            pltpu.VMEM((1, requests), jnp.int32),
            pltpu.SMEM((slots,), jnp.int32),
            pltpu.SMEM((slots,), jnp.int32),
            pltpu.VMEM(w_query.shape, jnp.bfloat16),
            pltpu.VMEM(w_key.shape, jnp.bfloat16),
            pltpu.VMEM(w_value.shape, jnp.bfloat16),
            pltpu.VMEM(w_out.shape, jnp.bfloat16),
            pltpu.VMEM((slots, span, head_dim), jnp.bfloat16),
            pltpu.VMEM((slots, span, head_dim), jnp.bfloat16),
            pltpu.VMEM((slots, head_dim, span), jnp.bfloat16),
            pltpu.VMEM((wide, slots, 2 * key_cols), jnp.float32),
            pltpu.VMEM((wide - 1, slots, 2 * key_cols), jnp.float32),
            pltpu.VMEM((q_chunks, wide, slots, q_width), jnp.float32),
            pltpu.VMEM((q_chunks, wide, slots, q_width), jnp.bfloat16),
            pltpu.VMEM((q_chunks, wide - 1, slots, q_width), jnp.bfloat16),
            pltpu.VMEM((heads_local * slots, head_dim), jnp.float32),
            pltpu.VMEM((kv_local, slots, group, span), jnp.float32),
            pltpu.VMEM((kv_local, slots, group * head_dim), jnp.bfloat16),
            pltpu.VMEM((kv_local, wide - 1, slots, group * head_dim), jnp.bfloat16),
            pltpu.VMEM((slots, group, head_dim), jnp.float32),
            pltpu.VMEM((requests, out_cols), jnp.float32),
            pltpu.VMEM((o_chunks, requests, o_width), jnp.bfloat16),
            pltpu.VMEM((o_chunks, narrow, requests, o_width), jnp.bfloat16),
            pltpu.SemaphoreType.DMA((5 + q_chunks + kv_local,)),
            pltpu.SemaphoreType.DMA((4,)),
            pltpu.SemaphoreType.DMA((4,)),
            pltpu.SemaphoreType.DMA((1 + q_chunks + kv_local + o_chunks,)),
        ],
        compiler_params=pltpu.CompilerParams(
            collective_id=0, has_side_effects=True, vmem_limit_bytes=main_kib * 1024
        ),
        name="decode_step",
    )(
        hidden,
        w_query,
        w_key,
        w_value,
        w_out,
        key_cache.reshape(slots, span, head_dim),
        value_cache.reshape(slots, span, head_dim),
        slot_of.reshape(1, requests),
        cycle_offset,
        valid_length,
    )
    return pl.pallas_call(
        finish,
        out_shape=outs,
        in_specs=[vmem] * 3,
        out_specs=(hbm,) * 3,
        scratch_shapes=[pltpu.SemaphoreType.DMA((3,))],
        compiler_params=pltpu.CompilerParams(vmem_limit_bytes=finish_kib * 1024),
        name="finish",
    )(*results)


def solution(mesh):
    placed = (
        P("groups", "wide"),
        P("wide", "narrow"),
        P("wide", "narrow"),
        P("wide", "narrow"),
        P("narrow", "wide"),
        P(("groups", "wide"), None, "narrow", None),
        P(("groups", "wide"), None, "narrow", None),
        P(("groups", "wide")),
        P(("groups", "wide")),
        P("groups"),
    )
    return jax.shard_map(
        functools.partial(per_device, mesh.shape["wide"], mesh.shape["narrow"]),
        mesh=mesh,
        in_specs=placed,
        out_specs=(
            P("groups", "wide"),
            P(("groups", "wide"), "narrow"),
            P(("groups", "wide"), "narrow"),
        ),
        check_vma=False,
    )
```

```python
import functools

import jax
import jax.numpy as jnp
from jax import lax
from jax.experimental import pallas as pl
from jax.experimental.pallas import tpu as pltpu
from jax.sharding import PartitionSpec as P

masked_low = -1e30
scope = jax.named_scope
MESH = pl.DeviceIdType.MESH
head_parts = 2
finish_kib = 1024
main_kib = 64512
o_most = 512
ahead = 7
meet_after = 0


def width_of(columns, most):
    width = min(columns, most)
    while columns % width:
        width -= 128
    return width


def blocks_of(columns, kv_local, wide):
    per_head = columns // kv_local
    parts = head_parts if wide <= 8 else 1
    width = width_of(per_head, max(per_head // parts // 128 * 128, 128))
    return tuple((col, width) for col in range(0, columns, width))


def kernel(
    wide,
    narrow,
    kv_local,
    q_blocks,
    o_width,
    hidden_in,
    w_query,
    w_key,
    w_value,
    w_out,
    key_cache,
    value_cache,
    slot_row_in,
    cycle_offset_in,
    valid_length_in,
    attn_out,
    new_keys,
    new_values,
    hidden,
    slot_row,
    cycle_offset,
    valid_length,
    wq,
    wkv,
    wo,
    keys,
    values,
    keys_across,
    kv_part,
    kv_got,
    q_own,
    q_part,
    q_got,
    queries,
    bias,
    heads_own,
    heads_got,
    heads_made,
    out_early,
    out_part,
    out_got,
    in_sem,
    small_sem,
    send_sem,
    recv_sem,
):
    me_wide = lax.axis_index("wide")
    me_narrow = lax.axis_index("narrow")
    requests = hidden.shape[0]
    slots = keys.shape[0]
    head_dim = keys.shape[2]
    span = keys.shape[1]
    window = span // kv_local
    query_cols = wq.shape[1]
    key_cols = new_keys.shape[1]
    out_cols = wo.shape[1]
    heads_local = query_cols // head_dim
    group = heads_local // kv_local
    group_cols = group * head_dim
    q_chunks = len(q_blocks)
    o_chunks = out_cols // o_width

    first = [
        pltpu.make_async_copy(w_key, wkv.at[:, pl.ds(0, key_cols)], in_sem.at[0]),
        pltpu.make_async_copy(w_value, wkv.at[:, pl.ds(key_cols, key_cols)], in_sem.at[0]),
    ]
    depth = wq.shape[0]
    pieces = [(col, width, 0, depth) for col, width in q_blocks]
    col, width = q_blocks[-1]
    half = depth // 32 * 16
    pieces[-1:] = [(col, width, 0, half), (col, width, half, depth - half)]
    for c, (col, width, row, count) in enumerate(pieces):
        part = (pl.ds(row, count), pl.ds(col, width))
        first.append(pltpu.make_async_copy(w_query.at[part], wq.at[part], in_sem.at[1 + c]))
    freed = [small_sem.at[0], small_sem.at[1], in_sem.at[0], in_sem.at[1]]
    freed += [in_sem.at[1 + len(pieces) + k] for k in range(max(kv_local - 2, 0))]
    cache_in = [
        pltpu.make_async_copy(key_cache, keys, freed[0]),
        pltpu.make_async_copy(value_cache, values, freed[1]),
    ]
    out_in = []
    for k in range(kv_local):
        span_k = pl.ds(k * group_cols, group_cols)
        out_in.append(
            pltpu.make_async_copy(w_out.at[span_k], wo.at[span_k], freed[2 + k])
        )
    small = [
        pltpu.make_async_copy(hidden_in, hidden, small_sem.at[0]),
        pltpu.make_async_copy(slot_row_in, slot_row, small_sem.at[1]),
        pltpu.make_async_copy(cycle_offset_in, cycle_offset, small_sem.at[2]),
        pltpu.make_async_copy(valid_length_in, valid_length, small_sem.at[3]),
    ]
    stream = first + cache_in + out_in
    for copy in small[:2]:
        copy.start()
    for copy in stream[:ahead]:
        copy.start(priority=1)
    for copy in small[2:]:
        copy.start()
    del stream[:ahead]

    barrier = pltpu.get_barrier_semaphore()
    peers = wide + narrow - 2
    for d in range(1, wide):
        pl.semaphore_signal(
            barrier,
            inc=1,
            device_id={"wide": lax.rem(me_wide + d, wide)},
            device_id_type=MESH,
        )
    for d in range(1, narrow):
        pl.semaphore_signal(
            barrier,
            inc=1,
            device_id={"narrow": lax.rem(me_narrow + d, narrow)},
            device_id_type=MESH,
        )

    with scope("pick"):
        small[0].wait()
        small[1].wait()
        slot_id = lax.broadcasted_iota(jnp.int32, (requests, requests), 0)
        pick = jnp.where(slot_row[...] == slot_id, 1.0, 0.0)
        rows = jnp.dot(
            pick.astype(jnp.bfloat16), hidden[...], preferred_element_type=jnp.float32
        ).astype(jnp.bfloat16)

    def to_owner(block, d):
        peer = lax.rem(me_wide + d, wide)
        part, got = (
            (kv_part, kv_got) if block == 0 else (q_part.at[block - 1], q_got.at[block - 1])
        )
        return pltpu.make_async_remote_copy(
            src_ref=part.at[peer],
            dst_ref=got.at[d - 1],
            send_sem=send_sem.at[min(block, 1)],
            recv_sem=recv_sem.at[0 if block == 0 else 1 + q_blocks[block - 1][0] // group_cols],
            device_id={"wide": peer},
            device_id_type=MESH,
        )

    def meets(sent, came, send, recv):
        return pltpu.make_async_remote_copy(
            src_ref=sent,
            dst_ref=came,
            send_sem=send,
            recv_sem=recv,
            device_id={"wide": lax.rem(me_wide + 1, wide)},
            device_id_type=MESH,
        )

    def by_owner(sums):
        return sums.reshape(wide, slots, sums.shape[1])

    def send(block):
        for d in range(1, wide):
            to_owner(block, d).start()

    def go(count):
        for _ in range(min(count, len(stream))):
            stream.pop(0).start(priority=1)

    with scope("kv_in"):
        pltpu.make_async_copy(wkv, wkv, in_sem.at[0]).wait()
    go(len(first) - ahead)
    with scope("kv_mm"):
        sums = jnp.dot(rows, wkv[...], preferred_element_type=jnp.float32)
        kv_part[...] = by_owner(sums)
    ready = [0]
    for c, (col, width, row, count) in enumerate(pieces):
        with scope("q_in%d" % c):
            first[2 + c].wait()
        if c >= len(pieces) - 3:
            go(1)
        with scope("q_mm%d" % c):
            sums = jnp.dot(
                rows[:, row : row + count],
                wq[row : row + count, col : col + width],
                preferred_element_type=jnp.float32,
            )
            if row > 0:
                sums = sums + early
            early = sums
            block = col // width
            if row + count == depth:
                for w in range(wide):
                    q_part[block, w] = sums[w * slots : (w + 1) * slots].astype(jnp.bfloat16)
        if row + count == depth:
            ready.append(1 + block)
        if c == min(meet_after, len(pieces) - 1):
            with scope("meet"):
                pl.semaphore_wait(barrier, peers)
        if c >= min(meet_after, len(pieces) - 1):
            while ready:
                send(ready.pop(0))
        if row + count == depth:
            q_own[block] = by_owner(sums)
    go(len(stream))

    with scope("mask"):
        place = lax.broadcasted_iota(jnp.int32, (group, span), 1)
        position = place // kv_local
        kv_of = place - position * kv_local
        scale = 1.0 / jnp.sqrt(jnp.float32(head_dim))
        for copy in small[2:]:
            copy.wait()
        for s in range(slots):
            distance = cycle_offset[s] - position
            distance = jnp.where(distance < 0, distance + window, distance)
            usable = (distance > 0) & (distance < valid_length[s])
            for k in range(kv_local):
                bias[k, s] = jnp.where(usable & (kv_of == k), 0.0, masked_low)

    with scope("keys_in"):
        cache_in[0].wait()
    with scope("turn"):
        for s in range(slots):
            keys_across[s] = keys[s].T

    def summed(own, got):
        total = own[me_wide]
        for d in range(1, wide):
            total = total + got[d - 1].astype(jnp.float32)
        return total

    per_head = q_chunks // kv_local

    def arrived(k):
        if wide > 1:
            came = kv_got if k < 0 else q_got.at[pl.ds(k * per_head, per_head)]
            meets(came, came, send_sem.at[0], recv_sem.at[1 + k]).wait_recv()

    with scope("sum_kv"):
        arrived(-1)
        if wide > 1:
            meets(kv_got, kv_got, send_sem.at[0], recv_sem.at[0]).wait_send()
        fresh = summed(kv_part, kv_got).astype(jnp.bfloat16)
        new_keys[...] = fresh[:, :key_cols]
        new_values[...] = fresh[:, key_cols:]
        fresh = fresh.astype(jnp.float32)

    def to_wide(k, i):
        peer = i + (i - me_wide + wide) // wide
        back = lax.rem(peer - me_wide + wide, wide)
        return pltpu.make_async_remote_copy(
            src_ref=heads_own.at[k],
            dst_ref=heads_got.at[k, back - 1],
            send_sem=send_sem.at[0],
            recv_sem=recv_sem.at[1 + kv_local + k],
            device_id={"wide": peer},
            device_id_type=MESH,
        )

    for k in range(kv_local):
        with scope("sum_q%d" % k):
            arrived(k)
            for block, (col, width) in enumerate(q_blocks):
                if col // group_cols == k:
                    sums = summed(q_own.at[block], q_got.at[block])
                    for t in range(width // head_dim):
                        row = (col // head_dim + t) * slots
                        queries[row : row + slots] = sums[:, t * head_dim : (t + 1) * head_dim]
        if k == 0:
            with scope("values_in"):
                cache_in[1].wait()
        with scope("attend%d" % k):
            query, scores, weights, own_weight, inverse = [], [], [], [], []
            for s in range(slots):
                query.append(
                    queries[pl.ds(k * group * slots + s, group, stride=slots), :].astype(
                        jnp.bfloat16
                    )
                )
                scores.append(
                    jnp.dot(query[s], keys_across[s], preferred_element_type=jnp.float32)
                )
            for s in range(slots):
                new_key = fresh[s : s + 1, k * head_dim : (k + 1) * head_dim]
                own_score = (
                    jnp.sum(query[s].astype(jnp.float32) * new_key, axis=1, keepdims=True) * scale
                )
                masked = scores[s] * scale + bias[k, s]
                top = jnp.maximum(jnp.max(masked, axis=1, keepdims=True), own_score)
                spread = jnp.exp(masked - top)
                own = jnp.exp(own_score - top)
                inverse.append(1.0 / (jnp.sum(spread, axis=1, keepdims=True) + own))
                weights.append(spread.astype(jnp.bfloat16))
                own_weight.append(own)
            for s in range(slots):
                col = key_cols + k * head_dim
                new_value = fresh[s : s + 1, col : col + head_dim]
                mixed = jnp.dot(weights[s], values[s], preferred_element_type=jnp.float32)
                heads_made[s] = (mixed + own_weight[s] * new_value) * inverse[s]
            heads_own[k] = jnp.concatenate(
                [heads_made[:, h, :] for h in range(group)], axis=1
            ).astype(jnp.bfloat16)
        for i in range(wide - 1):
            to_wide(k, i).start()

    if wide > 1:
        meets(q_got, q_got, send_sem.at[1], recv_sem.at[0]).wait_send()
    held_row = lax.broadcasted_iota(jnp.int32, (requests, requests), 0)
    back = held_row // slots
    held_slot = lax.rem(me_wide - back + wide, wide) * slots + (held_row - back * slots)
    give = jnp.where(slot_row[...] == held_slot, 1.0, 0.0).astype(jnp.bfloat16)

    def gathered(k):
        if wide > 1:
            came = heads_got.at[k]
            meets(came, came, send_sem.at[0], recv_sem.at[1 + kv_local + k]).wait_recv()
        by_slot = jnp.concatenate(
            [heads_own[k].astype(jnp.float32)]
            + [heads_got[k, d - 1].astype(jnp.float32) for d in range(1, wide)],
            axis=0,
        ).astype(jnp.bfloat16)
        return lax.dot_general(
            give,
            by_slot,
            (((0,), (0,)), ((), ())),
            preferred_element_type=jnp.float32,
        ).astype(jnp.bfloat16)

    if narrow == 4:
        others = [
            lax.rem(me_narrow + 2, 4),
            3 - me_narrow,
            me_narrow + 1 - 2 * lax.rem(me_narrow, 2),
        ]
    else:
        others = [lax.rem(me_narrow + d, narrow) for d in range(1, narrow)]

    def to_narrow(c, peer):
        return pltpu.make_async_remote_copy(
            src_ref=out_part.at[c],
            dst_ref=out_got.at[c, me_narrow],
            send_sem=send_sem.at[1],
            recv_sem=recv_sem.at[1 + 2 * kv_local + c // 2],
            device_id={"narrow": peer},
            device_id_type=MESH,
        )

    for k in range(kv_local):
        with scope("gather%d" % k):
            heads = gathered(k)
        with scope("out_in%d" % k):
            out_in[k].wait()
        with scope("project%d" % k):
            span_k = slice(k * group_cols, (k + 1) * group_cols)

            def product(c):
                cols = slice(c * o_width, (c + 1) * o_width)
                sums = jnp.dot(heads, wo[span_k, cols], preferred_element_type=jnp.float32)
                return sums + out_early[:, cols] if k > 0 else sums

            if k < kv_local - 1:
                for c in range(o_chunks):
                    out_early[:, c * o_width : (c + 1) * o_width] = product(c)
            else:
                after = product(0)
                for c in range(o_chunks):
                    sums = after
                    if c + 1 < o_chunks:
                        after = product(c + 1)
                    out_part[c] = sums.astype(jnp.bfloat16)
                    out_got[c, me_narrow] = sums.astype(jnp.bfloat16)
                    for peer in others[:1]:
                        to_narrow(c, peer).start()
                for peer in others[1:]:
                    for c in range(o_chunks):
                        to_narrow(c, peer).start()
    with scope("total"):
        for c in range(o_chunks):
            cols = slice(c * o_width, (c + 1) * o_width)
            if narrow > 1 and c % 2 == 0:
                came = out_got.at[pl.ds(c, min(2, o_chunks - c)), pl.ds(0, narrow - 1)]
                meets(came, came, send_sem.at[1], recv_sem.at[1 + 2 * kv_local + c // 2]).wait_recv()
            total = out_got[c, 0].astype(jnp.float32)
            for n in range(1, narrow):
                total = total + out_got[c, n].astype(jnp.float32)
            attn_out[:, cols] = total.astype(jnp.bfloat16)

    with scope("sent"):
        if wide > 1:
            meets(heads_got, heads_got, send_sem.at[0], recv_sem.at[0]).wait_send()
        if narrow > 1:
            gone = out_got.at[:, pl.ds(0, narrow - 1)]
            meets(gone, gone, send_sem.at[1], recv_sem.at[0]).wait_send()


def finish(attn, keys_new, values_new, attn_out, new_keys, new_values):
    attn_out[...] = attn[...]
    new_keys[...] = keys_new[...]
    new_values[...] = values_new[...]


def per_device(
    wide,
    narrow,
    hidden,
    w_query,
    w_key,
    w_value,
    w_out,
    key_cache,
    value_cache,
    cycle_offset,
    valid_length,
    slot_of,
):
    requests = slot_of.shape[0]
    slots, window, kv_local, head_dim = key_cache.shape
    query_cols = w_query.shape[1]
    key_cols = w_key.shape[1]
    out_cols = w_out.shape[1]
    q_blocks = blocks_of(query_cols, kv_local, wide)
    o_width = width_of(out_cols, o_most)
    q_chunks = len(q_blocks)
    o_chunks = out_cols // o_width
    q_width = q_blocks[0][1]
    span = window * kv_local
    vmem = pl.BlockSpec(memory_space=pltpu.VMEM)
    hbm = pl.BlockSpec(memory_space=pltpu.HBM)
    heads_local = query_cols // head_dim
    group = heads_local // kv_local
    outs = (
        jax.ShapeDtypeStruct((requests, out_cols), jnp.bfloat16),
        jax.ShapeDtypeStruct((slots, key_cols), jnp.bfloat16),
        jax.ShapeDtypeStruct((slots, key_cols), jnp.bfloat16),
    )
    results = pl.pallas_call(
        functools.partial(kernel, wide, narrow, kv_local, q_blocks, o_width),
        out_shape=tuple(pltpu.VMEM(out.shape, out.dtype) for out in outs),
        in_specs=[hbm] * 10,
        out_specs=(vmem, vmem, vmem),
        scratch_shapes=[
            pltpu.VMEM(hidden.shape, jnp.bfloat16),
            pltpu.VMEM((1, requests), jnp.int32),
            pltpu.SMEM((slots,), jnp.int32),
            pltpu.SMEM((slots,), jnp.int32),
            pltpu.VMEM(w_query.shape, jnp.bfloat16),
            pltpu.VMEM((w_key.shape[0], 2 * key_cols), jnp.bfloat16),
            pltpu.VMEM(w_out.shape, jnp.bfloat16),
            pltpu.VMEM((slots, span, head_dim), jnp.bfloat16),
            pltpu.VMEM((slots, span, head_dim), jnp.bfloat16),
            pltpu.VMEM((slots, head_dim, span), jnp.bfloat16),
            pltpu.VMEM((wide, slots, 2 * key_cols), jnp.float32),
            pltpu.VMEM((wide - 1, slots, 2 * key_cols), jnp.float32),
            pltpu.VMEM((q_chunks, wide, slots, q_width), jnp.float32),
            pltpu.VMEM((q_chunks, wide, slots, q_width), jnp.bfloat16),
            pltpu.VMEM((q_chunks, wide - 1, slots, q_width), jnp.bfloat16),
            pltpu.VMEM((heads_local * slots, head_dim), jnp.float32),
            pltpu.VMEM((kv_local, slots, group, span), jnp.float32),
            pltpu.VMEM((kv_local, slots, group * head_dim), jnp.bfloat16),
            pltpu.VMEM((kv_local, wide - 1, slots, group * head_dim), jnp.bfloat16),
            pltpu.VMEM((slots, group, head_dim), jnp.float32),
            pltpu.VMEM((requests, out_cols), jnp.float32),
            pltpu.VMEM((o_chunks, requests, o_width), jnp.bfloat16),
            pltpu.VMEM((o_chunks, narrow, requests, o_width), jnp.bfloat16),
            pltpu.SemaphoreType.DMA((2 + q_chunks + max(kv_local - 2, 0),)),
            pltpu.SemaphoreType.DMA((4,)),
            pltpu.SemaphoreType.DMA((2,)),
            pltpu.SemaphoreType.DMA((1 + 2 * kv_local + (o_chunks + 1) // 2,)),
        ],
        compiler_params=pltpu.CompilerParams(
            collective_id=0, has_side_effects=True, vmem_limit_bytes=main_kib * 1024
        ),
        name="decode_step",
    )(
        hidden,
        w_query,
        w_key,
        w_value,
        w_out,
        key_cache.reshape(slots, span, head_dim),
        value_cache.reshape(slots, span, head_dim),
        slot_of.reshape(1, requests),
        cycle_offset,
        valid_length,
    )
    return pl.pallas_call(
        finish,
        out_shape=outs,
        in_specs=[vmem] * 3,
        out_specs=(vmem,) * 3,
        compiler_params=pltpu.CompilerParams(vmem_limit_bytes=finish_kib * 1024),
        name="finish",
    )(*results)


def solution(mesh):
    placed = (
        P("groups", "wide"),
        P("wide", "narrow"),
        P("wide", "narrow"),
        P("wide", "narrow"),
        P("narrow", "wide"),
        P(("groups", "wide"), None, "narrow", None),
        P(("groups", "wide"), None, "narrow", None),
        P(("groups", "wide")),
        P(("groups", "wide")),
        P("groups"),
    )
    return jax.shard_map(
        functools.partial(per_device, mesh.shape["wide"], mesh.shape["narrow"]),
        mesh=mesh,
        in_specs=placed,
        out_specs=(
            P("groups", "wide"),
            P(("groups", "wide"), "narrow"),
            P(("groups", "wide"), "narrow"),
        ),
        check_vma=False,
    )
```

```python
import functools

import jax
import jax.numpy as jnp
from jax import lax
from jax.experimental import pallas as pl
from jax.experimental.pallas import tpu as pltpu
from jax.sharding import PartitionSpec as P

masked_low = -1e30
scope = jax.named_scope
MESH = pl.DeviceIdType.MESH
head_parts = 2
finish_kib = 1024
main_kib = 64512
o_most = 512
ahead = 7
meet_after = 0


def width_of(columns, most):
    width = min(columns, most)
    while columns % width:
        width -= 128
    return width


def blocks_of(columns, kv_local, wide):
    per_head = columns // kv_local
    parts = head_parts if wide <= 8 else 1
    width = width_of(per_head, max(per_head // parts // 128 * 128, 128))
    return tuple((col, width) for col in range(0, columns, width))


def kernel(
    wide,
    narrow,
    kv_local,
    q_blocks,
    o_width,
    hidden_in,
    w_query,
    w_key,
    w_value,
    w_out,
    key_cache,
    value_cache,
    slot_row_in,
    cycle_offset_in,
    valid_length_in,
    attn_out,
    new_keys,
    new_values,
    hidden,
    slot_row,
    cycle_offset,
    valid_length,
    wq,
    wkv,
    wo,
    keys,
    values,
    keys_across,
    kv_part,
    kv_got,
    q_own,
    q_part,
    q_got,
    queries,
    bias,
    heads_own,
    heads_got,
    heads_made,
    out_early,
    out_part,
    out_got,
    in_sem,
    small_sem,
    send_sem,
    recv_sem,
):
    me_wide = lax.axis_index("wide")
    me_narrow = lax.axis_index("narrow")
    requests = hidden.shape[0]
    slots = keys.shape[0]
    head_dim = keys.shape[2]
    span = keys.shape[1]
    window = span // kv_local
    query_cols = wq.shape[1]
    key_cols = new_keys.shape[1]
    out_cols = wo.shape[1]
    heads_local = query_cols // head_dim
    group = heads_local // kv_local
    group_cols = group * head_dim
    q_chunks = len(q_blocks)
    o_chunks = out_cols // o_width

    first = [
        pltpu.make_async_copy(w_key, wkv.at[:, pl.ds(0, key_cols)], in_sem.at[0]),
        pltpu.make_async_copy(w_value, wkv.at[:, pl.ds(key_cols, key_cols)], in_sem.at[0]),
    ]
    depth = wq.shape[0]
    pieces = [(col, width, 0, depth) for col, width in q_blocks]
    col, width = q_blocks[-1]
    half = depth // 32 * 16
    pieces[-1:] = [(col, width, 0, half), (col, width, half, depth - half)]
    for c, (col, width, row, count) in enumerate(pieces):
        part = (pl.ds(row, count), pl.ds(col, width))
        first.append(pltpu.make_async_copy(w_query.at[part], wq.at[part], in_sem.at[1 + c]))
    freed = [small_sem.at[0], small_sem.at[1], in_sem.at[0], in_sem.at[1]]
    freed += [in_sem.at[1 + len(pieces) + k] for k in range(max(kv_local - 2, 0))]
    cache_in = [
        pltpu.make_async_copy(key_cache, keys, freed[0]),
        pltpu.make_async_copy(value_cache, values, freed[1]),
    ]
    out_in = []
    for k in range(kv_local):
        span_k = pl.ds(k * group_cols, group_cols)
        out_in.append(
            pltpu.make_async_copy(w_out.at[span_k], wo.at[span_k], freed[2 + k])
        )
    small = [
        pltpu.make_async_copy(hidden_in, hidden, small_sem.at[0]),
        pltpu.make_async_copy(slot_row_in, slot_row, small_sem.at[1]),
        pltpu.make_async_copy(cycle_offset_in, cycle_offset, small_sem.at[2]),
        pltpu.make_async_copy(valid_length_in, valid_length, small_sem.at[3]),
    ]
    stream = first + cache_in + out_in
    for copy in small[:2]:
        copy.start()
    for copy in stream[:ahead]:
        copy.start(priority=1)
    for copy in small[2:]:
        copy.start()
    del stream[:ahead]

    barrier = pltpu.get_barrier_semaphore()
    peers = wide + narrow - 2
    for d in range(1, wide):
        pl.semaphore_signal(
            barrier,
            inc=1,
            device_id={"wide": lax.rem(me_wide + d, wide)},
            device_id_type=MESH,
        )
    for d in range(1, narrow):
        pl.semaphore_signal(
            barrier,
            inc=1,
            device_id={"narrow": lax.rem(me_narrow + d, narrow)},
            device_id_type=MESH,
        )

    with scope("pick"):
        small[0].wait()
        small[1].wait()
        slot_id = lax.broadcasted_iota(jnp.int32, (requests, requests), 0)
        pick = jnp.where(slot_row[...] == slot_id, 1.0, 0.0)
        rows = jnp.dot(
            pick.astype(jnp.bfloat16), hidden[...], preferred_element_type=jnp.float32
        ).astype(jnp.bfloat16)

    def to_owner(block, d):
        peer = lax.rem(me_wide + d, wide)
        part, got = (
            (kv_part, kv_got) if block == 0 else (q_part.at[block - 1], q_got.at[block - 1])
        )
        return pltpu.make_async_remote_copy(
            src_ref=part.at[peer],
            dst_ref=got.at[d - 1],
            send_sem=send_sem.at[min(block, 1)],
            recv_sem=recv_sem.at[0 if block == 0 else 1 + q_blocks[block - 1][0] // group_cols],
            device_id={"wide": peer},
            device_id_type=MESH,
        )

    def meets(sent, came, send, recv):
        return pltpu.make_async_remote_copy(
            src_ref=sent,
            dst_ref=came,
            send_sem=send,
            recv_sem=recv,
            device_id={"wide": lax.rem(me_wide + 1, wide)},
            device_id_type=MESH,
        )

    def by_owner(sums):
        return sums.reshape(wide, slots, sums.shape[1])

    def send(block):
        for d in range(1, wide):
            to_owner(block, d).start()

    def go(count):
        for _ in range(min(count, len(stream))):
            stream.pop(0).start(priority=1)

    with scope("kv_in"):
        pltpu.make_async_copy(wkv, wkv, in_sem.at[0]).wait()
    go(len(first) - ahead)
    with scope("kv_mm"):
        sums = jnp.dot(rows, wkv[...], preferred_element_type=jnp.float32)
        kv_part[...] = by_owner(sums)
    ready = [0]
    for c, (col, width, row, count) in enumerate(pieces):
        with scope("q_in%d" % c):
            first[2 + c].wait()
        if c >= len(pieces) - 3:
            go(1)
        with scope("q_mm%d" % c):
            sums = jnp.dot(
                rows[:, row : row + count],
                wq[row : row + count, col : col + width],
                preferred_element_type=jnp.float32,
            )
            if row > 0:
                sums = sums + early
            early = sums
            block = col // width
            if row + count == depth:
                for w in range(wide):
                    q_part[block, w] = sums[w * slots : (w + 1) * slots].astype(jnp.bfloat16)
        if row + count == depth:
            ready.append(1 + block)
        if c == min(meet_after, len(pieces) - 1):
            with scope("meet"):
                pl.semaphore_wait(barrier, peers)
        if c >= min(meet_after, len(pieces) - 1):
            while ready:
                send(ready.pop(0))
        if row + count == depth:
            q_own[block] = by_owner(sums)
    go(len(stream))

    with scope("mask"):
        place = lax.broadcasted_iota(jnp.int32, (group, span), 1)
        position = place // kv_local
        kv_of = place - position * kv_local
        scale = 1.0 / jnp.sqrt(jnp.float32(head_dim))
        for copy in small[2:]:
            copy.wait()
        for s in range(slots):
            distance = cycle_offset[s] - position
            distance = jnp.where(distance < 0, distance + window, distance)
            usable = (distance > 0) & (distance < valid_length[s])
            for k in range(kv_local):
                bias[k, s] = jnp.where(usable & (kv_of == k), 0.0, masked_low)

    with scope("keys_in"):
        cache_in[0].wait()
    with scope("turn"):
        for s in range(slots):
            keys_across[s] = keys[s].T

    def summed(own, got):
        total = own[me_wide]
        for d in range(1, wide):
            total = total + got[d - 1].astype(jnp.float32)
        return total

    per_head = q_chunks // kv_local

    def arrived(k):
        if wide > 1:
            came = kv_got if k < 0 else q_got.at[pl.ds(k * per_head, per_head)]
            meets(came, came, send_sem.at[0], recv_sem.at[1 + k]).wait_recv()

    with scope("sum_kv"):
        arrived(-1)
        if wide > 1:
            meets(kv_got, kv_got, send_sem.at[0], recv_sem.at[0]).wait_send()
        fresh = summed(kv_part, kv_got).astype(jnp.bfloat16)
        new_keys[...] = fresh[:, :key_cols]
        new_values[...] = fresh[:, key_cols:]
        fresh = fresh.astype(jnp.float32)

    def to_wide(k, i):
        peer = i + (i - me_wide + wide) // wide
        back = lax.rem(peer - me_wide + wide, wide)
        return pltpu.make_async_remote_copy(
            src_ref=heads_own.at[k],
            dst_ref=heads_got.at[k, back - 1],
            send_sem=send_sem.at[0],
            recv_sem=recv_sem.at[1 + kv_local + k],
            device_id={"wide": peer},
            device_id_type=MESH,
        )

    for k in range(kv_local):
        with scope("sum_q%d" % k):
            arrived(k)
            for block, (col, width) in enumerate(q_blocks):
                if col // group_cols == k:
                    sums = summed(q_own.at[block], q_got.at[block])
                    for t in range(width // head_dim):
                        row = (col // head_dim + t) * slots
                        queries[row : row + slots] = sums[:, t * head_dim : (t + 1) * head_dim]
        if k == 0:
            with scope("values_in"):
                cache_in[1].wait()
        with scope("attend%d" % k):
            query, scores, weights, own_weight, inverse = [], [], [], [], []
            for s in range(slots):
                query.append(
                    queries[pl.ds(k * group * slots + s, group, stride=slots), :].astype(
                        jnp.bfloat16
                    )
                )
                scores.append(
                    jnp.dot(query[s], keys_across[s], preferred_element_type=jnp.float32)
                )
            for s in range(slots):
                new_key = fresh[s : s + 1, k * head_dim : (k + 1) * head_dim]
                own_score = (
                    jnp.sum(query[s].astype(jnp.float32) * new_key, axis=1, keepdims=True) * scale
                )
                masked = scores[s] * scale + bias[k, s]
                top = jnp.maximum(jnp.max(masked, axis=1, keepdims=True), own_score)
                spread = jnp.exp(masked - top)
                own = jnp.exp(own_score - top)
                inverse.append(1.0 / (jnp.sum(spread, axis=1, keepdims=True) + own))
                weights.append(spread.astype(jnp.bfloat16))
                own_weight.append(own)
            for s in range(slots):
                col = key_cols + k * head_dim
                new_value = fresh[s : s + 1, col : col + head_dim]
                mixed = jnp.dot(weights[s], values[s], preferred_element_type=jnp.float32)
                heads_made[s] = (mixed + own_weight[s] * new_value) * inverse[s]
            heads_own[k] = jnp.concatenate(
                [heads_made[:, h, :] for h in range(group)], axis=1
            ).astype(jnp.bfloat16)
        for i in range(wide - 1):
            to_wide(k, i).start()

    if wide > 1:
        meets(q_got, q_got, send_sem.at[1], recv_sem.at[0]).wait_send()
    held_row = lax.broadcasted_iota(jnp.int32, (requests, requests), 0)
    back = held_row // slots
    held_slot = lax.rem(me_wide - back + wide, wide) * slots + (held_row - back * slots)
    give = jnp.where(slot_row[...] == held_slot, 1.0, 0.0)
    take = give.T.astype(jnp.bfloat16)

    def gathered(k):
        if wide > 1:
            came = heads_got.at[k]
            meets(came, came, send_sem.at[0], recv_sem.at[1 + kv_local + k]).wait_recv()
        by_slot = jnp.concatenate(
            [heads_own[k]] + [heads_got[k, d - 1] for d in range(1, wide)], axis=0
        )
        return jnp.dot(take, by_slot, preferred_element_type=jnp.float32).astype(jnp.bfloat16)

    if narrow == 4:
        others = [
            lax.rem(me_narrow + 2, 4),
            3 - me_narrow,
            me_narrow + 1 - 2 * lax.rem(me_narrow, 2),
        ]
    else:
        others = [lax.rem(me_narrow + d, narrow) for d in range(1, narrow)]

    def to_narrow(c, peer):
        return pltpu.make_async_remote_copy(
            src_ref=out_part.at[c],
            dst_ref=out_got.at[c, me_narrow],
            send_sem=send_sem.at[1],
            recv_sem=recv_sem.at[1 + 2 * kv_local + c // 2],
            device_id={"narrow": peer},
            device_id_type=MESH,
        )

    for k in range(kv_local):
        with scope("gather%d" % k):
            heads = gathered(k)
        with scope("out_in%d" % k):
            out_in[k].wait()
        with scope("project%d" % k):
            span_k = slice(k * group_cols, (k + 1) * group_cols)

            def product(c):
                cols = slice(c * o_width, (c + 1) * o_width)
                sums = jnp.dot(heads, wo[span_k, cols], preferred_element_type=jnp.float32)
                return sums + out_early[:, cols] if k > 0 else sums

            if k < kv_local - 1:
                for c in range(o_chunks):
                    out_early[:, c * o_width : (c + 1) * o_width] = product(c)
            else:
                after = product(0)
                for c in range(o_chunks):
                    sums = after
                    if c + 1 < o_chunks:
                        after = product(c + 1)
                    out_part[c] = sums.astype(jnp.bfloat16)
                    out_got[c, me_narrow] = sums.astype(jnp.bfloat16)
                    for peer in others[:1]:
                        to_narrow(c, peer).start()
                for peer in others[1:]:
                    for c in range(o_chunks):
                        to_narrow(c, peer).start()
    with scope("total"):
        for c in range(o_chunks):
            cols = slice(c * o_width, (c + 1) * o_width)
            if narrow > 1 and c % 2 == 0:
                came = out_got.at[pl.ds(c, min(2, o_chunks - c)), pl.ds(0, narrow - 1)]
                meets(came, came, send_sem.at[1], recv_sem.at[1 + 2 * kv_local + c // 2]).wait_recv()
            total = out_got[c, 0].astype(jnp.float32)
            for n in range(1, narrow):
                total = total + out_got[c, n].astype(jnp.float32)
            attn_out[:, cols] = total.astype(jnp.bfloat16)

    with scope("sent"):
        if wide > 1:
            meets(heads_got, heads_got, send_sem.at[0], recv_sem.at[0]).wait_send()
        if narrow > 1:
            gone = out_got.at[:, pl.ds(0, narrow - 1)]
            meets(gone, gone, send_sem.at[1], recv_sem.at[0]).wait_send()


def finish(attn, keys_new, values_new, attn_out, new_keys, new_values):
    attn_out[...] = attn[...]
    new_keys[...] = keys_new[...]
    new_values[...] = values_new[...]


def per_device(
    wide,
    narrow,
    hidden,
    w_query,
    w_key,
    w_value,
    w_out,
    key_cache,
    value_cache,
    cycle_offset,
    valid_length,
    slot_of,
):
    requests = slot_of.shape[0]
    slots, window, kv_local, head_dim = key_cache.shape
    query_cols = w_query.shape[1]
    key_cols = w_key.shape[1]
    out_cols = w_out.shape[1]
    q_blocks = blocks_of(query_cols, kv_local, wide)
    o_width = width_of(out_cols, o_most)
    q_chunks = len(q_blocks)
    o_chunks = out_cols // o_width
    q_width = q_blocks[0][1]
    span = window * kv_local
    vmem = pl.BlockSpec(memory_space=pltpu.VMEM)
    hbm = pl.BlockSpec(memory_space=pltpu.HBM)
    heads_local = query_cols // head_dim
    group = heads_local // kv_local
    outs = (
        jax.ShapeDtypeStruct((requests, out_cols), jnp.bfloat16),
        jax.ShapeDtypeStruct((slots, key_cols), jnp.bfloat16),
        jax.ShapeDtypeStruct((slots, key_cols), jnp.bfloat16),
    )
    results = pl.pallas_call(
        functools.partial(kernel, wide, narrow, kv_local, q_blocks, o_width),
        out_shape=tuple(pltpu.VMEM(out.shape, out.dtype) for out in outs),
        in_specs=[hbm] * 10,
        out_specs=(vmem, vmem, vmem),
        scratch_shapes=[
            pltpu.VMEM(hidden.shape, jnp.bfloat16),
            pltpu.VMEM((1, requests), jnp.int32),
            pltpu.SMEM((slots,), jnp.int32),
            pltpu.SMEM((slots,), jnp.int32),
            pltpu.VMEM(w_query.shape, jnp.bfloat16),
            pltpu.VMEM((w_key.shape[0], 2 * key_cols), jnp.bfloat16),
            pltpu.VMEM(w_out.shape, jnp.bfloat16),
            pltpu.VMEM((slots, span, head_dim), jnp.bfloat16),
            pltpu.VMEM((slots, span, head_dim), jnp.bfloat16),
            pltpu.VMEM((slots, head_dim, span), jnp.bfloat16),
            pltpu.VMEM((wide, slots, 2 * key_cols), jnp.float32),
            pltpu.VMEM((wide - 1, slots, 2 * key_cols), jnp.float32),
            pltpu.VMEM((q_chunks, wide, slots, q_width), jnp.float32),
            pltpu.VMEM((q_chunks, wide, slots, q_width), jnp.bfloat16),
            pltpu.VMEM((q_chunks, wide - 1, slots, q_width), jnp.bfloat16),
            pltpu.VMEM((heads_local * slots, head_dim), jnp.float32),
            pltpu.VMEM((kv_local, slots, group, span), jnp.float32),
            pltpu.VMEM((kv_local, slots, group * head_dim), jnp.bfloat16),
            pltpu.VMEM((kv_local, wide - 1, slots, group * head_dim), jnp.bfloat16),
            pltpu.VMEM((slots, group, head_dim), jnp.float32),
            pltpu.VMEM((requests, out_cols), jnp.float32),
            pltpu.VMEM((o_chunks, requests, o_width), jnp.bfloat16),
            pltpu.VMEM((o_chunks, narrow, requests, o_width), jnp.bfloat16),
            pltpu.SemaphoreType.DMA((2 + q_chunks + max(kv_local - 2, 0),)),
            pltpu.SemaphoreType.DMA((4,)),
            pltpu.SemaphoreType.DMA((2,)),
            pltpu.SemaphoreType.DMA((1 + 2 * kv_local + (o_chunks + 1) // 2,)),
        ],
        compiler_params=pltpu.CompilerParams(
            collective_id=0, has_side_effects=True, vmem_limit_bytes=main_kib * 1024
        ),
        name="decode_step",
    )(
        hidden,
        w_query,
        w_key,
        w_value,
        w_out,
        key_cache.reshape(slots, span, head_dim),
        value_cache.reshape(slots, span, head_dim),
        slot_of.reshape(1, requests),
        cycle_offset,
        valid_length,
    )
    return pl.pallas_call(
        finish,
        out_shape=outs,
        in_specs=[vmem] * 3,
        out_specs=(vmem,) * 3,
        compiler_params=pltpu.CompilerParams(vmem_limit_bytes=finish_kib * 1024),
        name="finish",
    )(*results)


def solution(mesh):
    placed = (
        P("groups", "wide"),
        P("wide", "narrow"),
        P("wide", "narrow"),
        P("wide", "narrow"),
        P("narrow", "wide"),
        P(("groups", "wide"), None, "narrow", None),
        P(("groups", "wide"), None, "narrow", None),
        P(("groups", "wide")),
        P(("groups", "wide")),
        P("groups"),
    )
    return jax.shard_map(
        functools.partial(per_device, mesh.shape["wide"], mesh.shape["narrow"]),
        mesh=mesh,
        in_specs=placed,
        out_specs=(
            P("groups", "wide"),
            P(("groups", "wide"), "narrow"),
            P(("groups", "wide"), "narrow"),
        ),
        check_vma=False,
    )
```

```python
import functools

import jax
import jax.numpy as jnp
from jax import lax
from jax.experimental import pallas as pl
from jax.experimental.pallas import tpu as pltpu
from jax.sharding import PartitionSpec as P

masked_low = -1e30
scope = jax.named_scope
MESH = pl.DeviceIdType.MESH
head_parts = 2
finish_kib = 1024
main_kib = 64512
o_most = 512
ahead = 7
meet_after = 0


def width_of(columns, most):
    width = min(columns, most)
    while columns % width:
        width -= 128
    return width


def blocks_of(columns, kv_local, wide):
    per_head = columns // kv_local
    parts = head_parts if wide <= 8 else 1
    width = width_of(per_head, max(per_head // parts // 128 * 128, 128))
    return tuple((col, width) for col in range(0, columns, width))


def kernel(
    wide,
    narrow,
    kv_local,
    q_blocks,
    o_width,
    hidden_in,
    w_query,
    w_key,
    w_value,
    w_out,
    key_cache,
    value_cache,
    slot_row_in,
    cycle_offset_in,
    valid_length_in,
    attn_out,
    new_keys,
    new_values,
    hidden,
    slot_row,
    cycle_offset,
    valid_length,
    wq,
    wkv,
    wo,
    keys,
    values,
    keys_across,
    kv_part,
    kv_got,
    q_own,
    q_part,
    q_got,
    queries,
    bias,
    heads_own,
    heads_got,
    heads_made,
    out_early,
    out_part,
    out_got,
    in_sem,
    small_sem,
    send_sem,
    recv_sem,
):
    me_wide = lax.axis_index("wide")
    me_narrow = lax.axis_index("narrow")
    requests = hidden.shape[0]
    slots = keys.shape[0]
    head_dim = keys.shape[2]
    span = keys.shape[1]
    window = span // kv_local
    query_cols = wq.shape[1]
    key_cols = new_keys.shape[1]
    out_cols = wo.shape[1]
    heads_local = query_cols // head_dim
    group = heads_local // kv_local
    group_cols = group * head_dim
    q_chunks = len(q_blocks)
    o_chunks = out_cols // o_width

    first = [
        pltpu.make_async_copy(w_key, wkv.at[:, pl.ds(0, key_cols)], in_sem.at[0]),
        pltpu.make_async_copy(w_value, wkv.at[:, pl.ds(key_cols, key_cols)], in_sem.at[0]),
    ]
    depth = wq.shape[0]
    pieces = [(col, width, 0, depth) for col, width in q_blocks]
    col, width = q_blocks[-1]
    half = depth // 32 * 16
    pieces[-1:] = [(col, width, 0, half), (col, width, half, depth - half)]
    for c, (col, width, row, count) in enumerate(pieces):
        part = (pl.ds(row, count), pl.ds(col, width))
        first.append(pltpu.make_async_copy(w_query.at[part], wq.at[part], in_sem.at[1 + c]))
    freed = [small_sem.at[0], small_sem.at[1], in_sem.at[0], in_sem.at[1]]
    freed += [in_sem.at[1 + len(pieces) + k] for k in range(max(kv_local - 2, 0))]
    cache_in = [
        pltpu.make_async_copy(key_cache, keys, freed[0]),
        pltpu.make_async_copy(value_cache, values, freed[1]),
    ]
    out_in = []
    for k in range(kv_local):
        span_k = pl.ds(k * group_cols, group_cols)
        out_in.append(
            pltpu.make_async_copy(w_out.at[span_k], wo.at[span_k], freed[2 + k])
        )
    small = [
        pltpu.make_async_copy(hidden_in, hidden, small_sem.at[0]),
        pltpu.make_async_copy(slot_row_in, slot_row, small_sem.at[1]),
        pltpu.make_async_copy(cycle_offset_in, cycle_offset, small_sem.at[2]),
        pltpu.make_async_copy(valid_length_in, valid_length, small_sem.at[3]),
    ]
    stream = first + cache_in + out_in
    for copy in small[:2]:
        copy.start()
    for copy in stream[:ahead]:
        copy.start(priority=1)
    for copy in small[2:]:
        copy.start()
    del stream[:ahead]

    barrier = pltpu.get_barrier_semaphore()
    peers = wide + narrow - 2
    for d in range(1, wide):
        pl.semaphore_signal(
            barrier,
            inc=1,
            device_id={"wide": lax.rem(me_wide + d, wide)},
            device_id_type=MESH,
        )
    for d in range(1, narrow):
        pl.semaphore_signal(
            barrier,
            inc=1,
            device_id={"narrow": lax.rem(me_narrow + d, narrow)},
            device_id_type=MESH,
        )

    with scope("pick"):
        small[0].wait()
        small[1].wait()
        slot_id = lax.broadcasted_iota(jnp.int32, (requests, requests), 0)
        pick = jnp.where(slot_row[...] == slot_id, 1.0, 0.0)
        rows = jnp.dot(
            pick.astype(jnp.bfloat16), hidden[...], preferred_element_type=jnp.float32
        ).astype(jnp.bfloat16)

    def to_owner(block, d):
        peer = lax.rem(me_wide + d, wide)
        part, got = (
            (kv_part, kv_got) if block == 0 else (q_part.at[block - 1], q_got.at[block - 1])
        )
        return pltpu.make_async_remote_copy(
            src_ref=part.at[peer],
            dst_ref=got.at[d - 1],
            send_sem=send_sem.at[min(block, 1)],
            recv_sem=recv_sem.at[0 if block == 0 else 1 + q_blocks[block - 1][0] // group_cols],
            device_id={"wide": peer},
            device_id_type=MESH,
        )

    def meets(sent, came, send, recv):
        return pltpu.make_async_remote_copy(
            src_ref=sent,
            dst_ref=came,
            send_sem=send,
            recv_sem=recv,
            device_id={"wide": lax.rem(me_wide + 1, wide)},
            device_id_type=MESH,
        )

    def by_owner(sums):
        return sums.reshape(wide, slots, sums.shape[1])

    def send(block):
        for d in range(1, wide):
            to_owner(block, d).start()

    def go(count):
        for _ in range(min(count, len(stream))):
            stream.pop(0).start(priority=1)

    with scope("kv_in"):
        pltpu.make_async_copy(wkv, wkv, in_sem.at[0]).wait()
    go(len(first) - ahead)
    with scope("kv_mm"):
        sums = jnp.dot(rows, wkv[...], preferred_element_type=jnp.float32)
        kv_part[...] = by_owner(sums)
    ready = [0]
    for c, (col, width, row, count) in enumerate(pieces):
        with scope("q_in%d" % c):
            first[2 + c].wait()
        if c >= len(pieces) - 3:
            go(1)
        with scope("q_mm%d" % c):
            sums = jnp.dot(
                rows[:, row : row + count],
                wq[row : row + count, col : col + width],
                preferred_element_type=jnp.float32,
            )
            if row > 0:
                sums = sums + early
            early = sums
            block = col // width
            if row + count == depth:
                for w in range(wide):
                    q_part[block, w] = sums[w * slots : (w + 1) * slots].astype(jnp.bfloat16)
        if row + count == depth:
            ready.append(1 + block)
        if c == min(meet_after, len(pieces) - 1):
            with scope("meet"):
                pl.semaphore_wait(barrier, peers)
        if c >= min(meet_after, len(pieces) - 1):
            while ready:
                send(ready.pop(0))
        if row + count == depth:
            q_own[block] = by_owner(sums)
    go(len(stream))

    with scope("mask"):
        place = lax.broadcasted_iota(jnp.int32, (group, span), 1)
        position = place // kv_local
        kv_of = place - position * kv_local
        scale = 1.0 / jnp.sqrt(jnp.float32(head_dim))
        for copy in small[2:]:
            copy.wait()
        for s in range(slots):
            distance = cycle_offset[s] - position
            distance = jnp.where(distance < 0, distance + window, distance)
            usable = (distance > 0) & (distance < valid_length[s])
            for k in range(kv_local):
                bias[k, s] = jnp.where(usable & (kv_of == k), 0.0, masked_low)

    with scope("keys_in"):
        cache_in[0].wait()
    with scope("turn"):
        for s in range(slots):
            keys_across[s] = keys[s].T

    def summed(own, got):
        total = own[me_wide]
        for d in range(1, wide):
            total = total + got[d - 1].astype(jnp.float32)
        return total

    per_head = q_chunks // kv_local

    def arrived(k):
        if wide > 1:
            came = kv_got if k < 0 else q_got.at[pl.ds(k * per_head, per_head)]
            meets(came, came, send_sem.at[0], recv_sem.at[1 + k]).wait_recv()

    with scope("sum_kv"):
        arrived(-1)
        if wide > 1:
            meets(kv_got, kv_got, send_sem.at[0], recv_sem.at[0]).wait_send()
        fresh = summed(kv_part, kv_got).astype(jnp.bfloat16)
        new_keys[...] = fresh[:, :key_cols]
        new_values[...] = fresh[:, key_cols:]
        fresh = fresh.astype(jnp.float32)

    def to_wide(k, i):
        peer = i + (i - me_wide + wide) // wide
        back = lax.rem(peer - me_wide + wide, wide)
        return pltpu.make_async_remote_copy(
            src_ref=heads_own.at[k],
            dst_ref=heads_got.at[k, back - 1],
            send_sem=send_sem.at[0],
            recv_sem=recv_sem.at[1 + kv_local + k],
            device_id={"wide": peer},
            device_id_type=MESH,
        )

    for k in range(kv_local):
        with scope("sum_q%d" % k):
            arrived(k)
            for block, (col, width) in enumerate(q_blocks):
                if col // group_cols == k:
                    sums = summed(q_own.at[block], q_got.at[block])
                    for t in range(width // head_dim):
                        row = (col // head_dim + t) * slots
                        queries[row : row + slots] = sums[:, t * head_dim : (t + 1) * head_dim]
        if k == 0:
            with scope("values_in"):
                cache_in[1].wait()
        with scope("attend%d" % k):
            query, scores, weights, own_weight, inverse = [], [], [], [], []
            for s in range(slots):
                query.append(
                    queries[pl.ds(k * group * slots + s, group, stride=slots), :].astype(
                        jnp.bfloat16
                    )
                )
                scores.append(
                    jnp.dot(query[s], keys_across[s], preferred_element_type=jnp.float32)
                )
            for s in range(slots):
                new_key = fresh[s : s + 1, k * head_dim : (k + 1) * head_dim]
                own_score = (
                    jnp.sum(query[s].astype(jnp.float32) * new_key, axis=1, keepdims=True) * scale
                )
                masked = scores[s] * scale + bias[k, s]
                top = jnp.maximum(jnp.max(masked, axis=1, keepdims=True), own_score)
                spread = jnp.exp(masked - top)
                own = jnp.exp(own_score - top)
                inverse.append(1.0 / (jnp.sum(spread, axis=1, keepdims=True) + own))
                weights.append(spread.astype(jnp.bfloat16))
                own_weight.append(own)
            for s in range(slots):
                col = key_cols + k * head_dim
                new_value = fresh[s : s + 1, col : col + head_dim]
                mixed = jnp.dot(weights[s], values[s], preferred_element_type=jnp.float32)
                heads_made[s] = (mixed + own_weight[s] * new_value) * inverse[s]
            heads_own[k] = jnp.concatenate(
                [heads_made[:, h, :] for h in range(group)], axis=1
            ).astype(jnp.bfloat16)
        for i in range(wide - 1):
            to_wide(k, i).start()

    if wide > 1:
        meets(q_got, q_got, send_sem.at[1], recv_sem.at[0]).wait_send()
    held_row = lax.broadcasted_iota(jnp.int32, (requests, requests), 0)
    back = held_row // slots
    held_slot = lax.rem(me_wide - back + wide, wide) * slots + (held_row - back * slots)
    give = jnp.where(slot_row[...] == held_slot, 1.0, 0.0)
    take = give.T.astype(jnp.bfloat16)

    def gathered(k):
        if wide > 1:
            came = heads_got.at[k]
            meets(came, came, send_sem.at[0], recv_sem.at[1 + kv_local + k]).wait_recv()
        by_slot = jnp.concatenate(
            [heads_own[k]] + [heads_got[k, d - 1] for d in range(1, wide)], axis=0
        )
        return jnp.dot(take, by_slot, preferred_element_type=jnp.float32).astype(jnp.bfloat16)

    if narrow == 4:
        others = [
            lax.rem(me_narrow + 2, 4),
            3 - me_narrow,
            me_narrow + 1 - 2 * lax.rem(me_narrow, 2),
        ]
    else:
        others = [lax.rem(me_narrow + d, narrow) for d in range(1, narrow)]

    def to_narrow(c, peer):
        return pltpu.make_async_remote_copy(
            src_ref=out_part.at[c],
            dst_ref=out_got.at[c, me_narrow],
            send_sem=send_sem.at[1],
            recv_sem=recv_sem.at[1 + 2 * kv_local + c // 2],
            device_id={"narrow": peer},
            device_id_type=MESH,
        )

    for k in range(kv_local):
        with scope("gather%d" % k):
            heads = gathered(k)
        with scope("out_in%d" % k):
            out_in[k].wait()
        with scope("project%d" % k):
            span_k = slice(k * group_cols, (k + 1) * group_cols)

            def product(c):
                cols = slice(c * o_width, (c + 1) * o_width)
                sums = jnp.dot(heads, wo[span_k, cols], preferred_element_type=jnp.float32)
                return sums + out_early[:, cols] if k > 0 else sums

            if k < kv_local - 1:
                out_early[...] = jnp.dot(
                    heads, wo[span_k], preferred_element_type=jnp.float32
                ) + (out_early[...] if k > 0 else 0.0)
            else:
                after = product(0)
                for c in range(o_chunks):
                    sums = after
                    if c + 1 < o_chunks:
                        after = product(c + 1)
                    out_part[c] = sums.astype(jnp.bfloat16)
                    out_got[c, me_narrow] = sums.astype(jnp.bfloat16)
                    for peer in others[:1]:
                        to_narrow(c, peer).start()
                for peer in others[1:]:
                    for c in range(o_chunks):
                        to_narrow(c, peer).start()
    with scope("total"):
        for c in range(o_chunks):
            cols = slice(c * o_width, (c + 1) * o_width)
            if narrow > 1 and c % 2 == 0:
                came = out_got.at[pl.ds(c, min(2, o_chunks - c)), pl.ds(0, narrow - 1)]
                meets(came, came, send_sem.at[1], recv_sem.at[1 + 2 * kv_local + c // 2]).wait_recv()
            total = out_got[c, 0].astype(jnp.float32)
            for n in range(1, narrow):
                total = total + out_got[c, n].astype(jnp.float32)
            attn_out[:, cols] = total.astype(jnp.bfloat16)

    with scope("sent"):
        if wide > 1:
            meets(heads_got, heads_got, send_sem.at[0], recv_sem.at[0]).wait_send()
        if narrow > 1:
            gone = out_got.at[:, pl.ds(0, narrow - 1)]
            meets(gone, gone, send_sem.at[1], recv_sem.at[0]).wait_send()


def finish(attn, keys_new, values_new, attn_out, new_keys, new_values):
    attn_out[...] = attn[...]
    new_keys[...] = keys_new[...]
    new_values[...] = values_new[...]


def per_device(
    wide,
    narrow,
    hidden,
    w_query,
    w_key,
    w_value,
    w_out,
    key_cache,
    value_cache,
    cycle_offset,
    valid_length,
    slot_of,
):
    requests = slot_of.shape[0]
    slots, window, kv_local, head_dim = key_cache.shape
    query_cols = w_query.shape[1]
    key_cols = w_key.shape[1]
    out_cols = w_out.shape[1]
    q_blocks = blocks_of(query_cols, kv_local, wide)
    o_width = width_of(out_cols, o_most)
    q_chunks = len(q_blocks)
    o_chunks = out_cols // o_width
    q_width = q_blocks[0][1]
    span = window * kv_local
    vmem = pl.BlockSpec(memory_space=pltpu.VMEM)
    hbm = pl.BlockSpec(memory_space=pltpu.HBM)
    heads_local = query_cols // head_dim
    group = heads_local // kv_local
    outs = (
        jax.ShapeDtypeStruct((requests, out_cols), jnp.bfloat16),
        jax.ShapeDtypeStruct((slots, key_cols), jnp.bfloat16),
        jax.ShapeDtypeStruct((slots, key_cols), jnp.bfloat16),
    )
    results = pl.pallas_call(
        functools.partial(kernel, wide, narrow, kv_local, q_blocks, o_width),
        out_shape=tuple(pltpu.VMEM(out.shape, out.dtype) for out in outs),
        in_specs=[hbm] * 10,
        out_specs=(vmem, vmem, vmem),
        scratch_shapes=[
            pltpu.VMEM(hidden.shape, jnp.bfloat16),
            pltpu.VMEM((1, requests), jnp.int32),
            pltpu.SMEM((slots,), jnp.int32),
            pltpu.SMEM((slots,), jnp.int32),
            pltpu.VMEM(w_query.shape, jnp.bfloat16),
            pltpu.VMEM((w_key.shape[0], 2 * key_cols), jnp.bfloat16),
            pltpu.VMEM(w_out.shape, jnp.bfloat16),
            pltpu.VMEM((slots, span, head_dim), jnp.bfloat16),
            pltpu.VMEM((slots, span, head_dim), jnp.bfloat16),
            pltpu.VMEM((slots, head_dim, span), jnp.bfloat16),
            pltpu.VMEM((wide, slots, 2 * key_cols), jnp.float32),
            pltpu.VMEM((wide - 1, slots, 2 * key_cols), jnp.float32),
            pltpu.VMEM((q_chunks, wide, slots, q_width), jnp.float32),
            pltpu.VMEM((q_chunks, wide, slots, q_width), jnp.bfloat16),
            pltpu.VMEM((q_chunks, wide - 1, slots, q_width), jnp.bfloat16),
            pltpu.VMEM((heads_local * slots, head_dim), jnp.float32),
            pltpu.VMEM((kv_local, slots, group, span), jnp.float32),
            pltpu.VMEM((kv_local, slots, group * head_dim), jnp.bfloat16),
            pltpu.VMEM((kv_local, wide - 1, slots, group * head_dim), jnp.bfloat16),
            pltpu.VMEM((slots, group, head_dim), jnp.float32),
            pltpu.VMEM((requests, out_cols), jnp.float32),
            pltpu.VMEM((o_chunks, requests, o_width), jnp.bfloat16),
            pltpu.VMEM((o_chunks, narrow, requests, o_width), jnp.bfloat16),
            pltpu.SemaphoreType.DMA((2 + q_chunks + max(kv_local - 2, 0),)),
            pltpu.SemaphoreType.DMA((4,)),
            pltpu.SemaphoreType.DMA((2,)),
            pltpu.SemaphoreType.DMA((1 + 2 * kv_local + (o_chunks + 1) // 2,)),
        ],
        compiler_params=pltpu.CompilerParams(
            collective_id=0, has_side_effects=True, vmem_limit_bytes=main_kib * 1024
        ),
        name="decode_step",
    )(
        hidden,
        w_query,
        w_key,
        w_value,
        w_out,
        key_cache.reshape(slots, span, head_dim),
        value_cache.reshape(slots, span, head_dim),
        slot_of.reshape(1, requests),
        cycle_offset,
        valid_length,
    )
    return pl.pallas_call(
        finish,
        out_shape=outs,
        in_specs=[vmem] * 3,
        out_specs=(vmem,) * 3,
        compiler_params=pltpu.CompilerParams(vmem_limit_bytes=finish_kib * 1024),
        name="finish",
    )(*results)


def solution(mesh):
    placed = (
        P("groups", "wide"),
        P("wide", "narrow"),
        P("wide", "narrow"),
        P("wide", "narrow"),
        P("narrow", "wide"),
        P(("groups", "wide"), None, "narrow", None),
        P(("groups", "wide"), None, "narrow", None),
        P(("groups", "wide")),
        P(("groups", "wide")),
        P("groups"),
    )
    return jax.shard_map(
        functools.partial(per_device, mesh.shape["wide"], mesh.shape["narrow"]),
        mesh=mesh,
        in_specs=placed,
        out_specs=(
            P("groups", "wide"),
            P(("groups", "wide"), "narrow"),
            P(("groups", "wide"), "narrow"),
        ),
        check_vma=False,
    )
```
